512 devices in a mesh: seq: 128 (over z, y, core), head: 4 (over x).
Axes of the slice: x: 4, y: 8, z: 8, core: 2. Of those that a mesh axis runs over, the one named last changes fastest.
Arguments:
- query_rows: bfloat16 [16384, 2048], P('seq', 'head'), may hold values from -10 to 10
- key_rows: bfloat16 [16384, 2048], P('seq', 'head'), may hold values from -10 to 10
- value_rows: bfloat16 [16384, 2048], P('seq', 'head'), may hold values from -6 to 6
- out_weight: bfloat16 [2048, 2048], P('head'), may hold values from -0.1875 to 0.1875
- cluster_ids: int32 [128, 16], P('seq'), may hold values from 0 to 127, as said below
Outputs:
- layer_out: bfloat16 [16384, 2048], P('seq', 'head')
The draws below stay inside these ranges and needn't reach their ends.
Inputs may be any that keep to these rules, and one draw needn't show every extreme that they name: `cluster_ids`: row d names the clusters of device d's blocks in order. One device names one cluster for at most 1 of its blocks; some cluster is named 1 times by every device, so its owner receives the most from every source. Cluster sizes are skewed.
All inputs are finite; a program needn't handle non-finite values.
Results may differ from the reference program's by a relative error of at most 0.01.
Values may be sent and summed in bfloat16 or wider, within the bound.
A program may use at most 64 MiB of HBM per device.

```python
import jax
import jax.numpy as jnp
from jax import lax

HEADS = 16
HD = 128
D = 2048
BLOCK = 8
WINDOW = 1024
BLK_DEV = 16
SLOT = 1
TOK_DEV = 128
TOKENS = 16384
N_SEQ = 128


def base_rows(key, salt):
    base = jax.random.normal(jax.random.fold_in(key, salt), (TOKENS, HEADS * HD), jnp.float32)
    base = jnp.clip(base, -4.0, 4.0)
    return base


def draw_query_rows(key, part):
    base = base_rows(key, 11)
    return jnp.clip(base, -10.0, 10.0).astype(jnp.bfloat16)


def draw_key_rows(key, part):
    base = base_rows(key, 23)
    return jnp.clip(base, -10.0, 10.0).astype(jnp.bfloat16)


def draw_cluster_ids(key, part):
    label_count = N_SEQ * SLOT
    hot_count = max(1, N_SEQ // 32)
    hot_order = jax.random.permutation(jax.random.fold_in(key, 5), N_SEQ)
    is_hot = jnp.zeros((N_SEQ,), jnp.int32).at[hot_order[:hot_count]].set(1)
    label_iota = jnp.arange(label_count, dtype=jnp.int32)
    block_iota = jnp.arange(BLK_DEV, dtype=jnp.int32)

    def one_device(device):
        dev_key = jax.random.fold_in(key, 1000 + device)
        random_part = jax.random.randint(jax.random.fold_in(dev_key, 1), (label_count,), 0, 65536, jnp.int32)
        scores = random_part * label_count + label_iota + is_hot[label_iota % N_SEQ] * (1 << 25)
        chosen = lax.top_k(scores, BLK_DEV)[1]
        order_part = jax.random.randint(jax.random.fold_in(dev_key, 2), (BLK_DEV,), 0, 65536, jnp.int32)
        shuffle = jnp.argsort(order_part * BLK_DEV + block_iota)
        return (chosen[shuffle] % N_SEQ).astype(jnp.int32)
    return jax.vmap(one_device)(jnp.arange(N_SEQ, dtype=jnp.int32))


def raised(values, rng, source, target, parts, factor):
    owner, partner = [(jnp.arange(values.shape[dim]) // (values.shape[dim] // parts)).reshape([-1 if axis == dim else 1 for axis in range(values.ndim)]) for dim in (source, target)]
    chosen = jax.random.permutation(rng, parts)[partner]
    strong = (owner == chosen) | (owner == (partner + parts // 2) % parts)
    return jnp.where(strong, factor * values, values)


def level_of(own_key, shape, pieces, least, top_value):
    factor_of = 1.0
    for axis_at, shards_of in pieces:
        heights = jax.random.uniform(jax.random.fold_in(jax.random.fold_in(own_key, 6), axis_at), (shards_of,), jnp.float32, least / len(pieces), top_value / len(pieces))
        factor_of = factor_of * jnp.repeat(jnp.exp(heights), shape[axis_at] // shards_of).reshape((-1,) + (1,) * (len(shape) - 1 - axis_at))
    return factor_of


def gaussian(stream_key, extent, scale, limit, pieces=(), kind=jnp.bfloat16):
    entries = scale * jax.random.normal(stream_key, extent, jnp.float32)
    if pieces:
        entries = entries * level_of(stream_key, extent, pieces, -0.22, 0.18)
    return jnp.clip(entries, -limit, limit).astype(kind)


def noise_with(own_key, extent, deviation, bound, cuts, heavy, kind=jnp.bfloat16):
    values = deviation * jax.random.normal(own_key, extent, jnp.float32)
    if cuts:
        values = values * level_of(own_key, extent, cuts, -0.22, 0.18)
    return jnp.clip(raised(values, jax.random.fold_in(own_key, 3), *heavy), -bound, bound).astype(kind)


def setup_inputs(seed: int = 0) -> dict:
    keys = jax.random.split(jax.random.key(seed), 6)
    query_rows = draw_query_rows(jax.random.fold_in(keys[5], 71), 0)
    key_rows = draw_key_rows(jax.random.fold_in(keys[5], 71), 0)
    value_rows = gaussian(keys[2], (TOKENS, D), 1.0, 6.0, ((0, 128), (1, 4)))
    out_weight = noise_with(keys[3], (D, D), D ** -0.5, 0.1875, ((0, 4),), (0, 1, 4, 2.0))
    cluster_ids = draw_cluster_ids(jax.random.fold_in(keys[5], 71), 0)
    return dict(query_rows=query_rows, key_rows=key_rows, value_rows=value_rows, out_weight=out_weight, cluster_ids=cluster_ids)


def attend(queries_h, keys_h, values_h, allowed):
    scores = jnp.einsum("qhd,khd->hqk", queries_h.astype(jnp.float32), keys_h.astype(jnp.float32)) * (HD ** -0.5)
    scores = jnp.where(allowed[None], scores, -1e30)
    largest = jnp.max(scores, axis=2, keepdims=True)
    weights_raw = jnp.where(allowed[None], jnp.exp(scores - largest), 0.0)
    weights = (weights_raw / jnp.sum(weights_raw, axis=2, keepdims=True)).astype(jnp.bfloat16)
    return jnp.einsum("hqk,khd->qhd", weights.astype(jnp.float32), values_h.astype(jnp.float32))


def reference(query_rows, key_rows, value_rows, out_weight, cluster_ids):
    tokens_all = query_rows.shape[0]
    width = HEADS * HD
    block_count = N_SEQ * BLK_DEV
    capacity = N_SEQ * SLOT
    block_cluster = cluster_ids.reshape(-1).astype(jnp.int32)
    block_index = jnp.arange(block_count, dtype=jnp.int32)
    offsets = jnp.arange(BLOCK, dtype=jnp.int32)
    eye_mask = jnp.eye(capacity * BLOCK, dtype=bool)

    def one_cluster(cluster, routed):
        order_key = jnp.where(block_cluster == cluster, block_index, block_count + block_index)
        chosen = jnp.argsort(order_key)[:capacity].astype(jnp.int32)
        member = block_cluster[chosen] == cluster
        row_ids = (chosen[:, None] * BLOCK + offsets[None, :]).reshape(-1).astype(jnp.int32)
        member_rows = jnp.repeat(member, BLOCK)
        allowed = (member_rows[None, :] & (row_ids[None, :] <= row_ids[:, None])) | eye_mask
        heads_q = query_rows[row_ids].reshape(-1, HEADS, HD)
        heads_k = key_rows[row_ids].reshape(-1, HEADS, HD)
        heads_v = value_rows[row_ids].reshape(-1, HEADS, HD)
        result = attend(heads_q, heads_k, heads_v, allowed).astype(jnp.bfloat16).reshape(-1, width)
        target = jnp.where(member_rows, row_ids, tokens_all).astype(jnp.int32)
        return routed.at[target].set(result, mode="drop")

    routed = lax.fori_loop(0, N_SEQ, one_cluster, jnp.zeros((tokens_all, width), jnp.bfloat16))

    pad_zero = jnp.zeros((WINDOW, width), jnp.bfloat16)
    keys_padded = jnp.concatenate([pad_zero, key_rows], axis=0)
    values_padded = jnp.concatenate([pad_zero, value_rows], axis=0)
    span = WINDOW + TOK_DEV
    query_pos = jnp.arange(TOK_DEV, dtype=jnp.int32)[:, None]
    key_rel = jnp.arange(span, dtype=jnp.int32)[None, :] - WINDOW

    def one_shard(shard_index):
        first_row = (shard_index * TOK_DEV).astype(jnp.int32)
        query_part = lax.dynamic_slice_in_dim(query_rows, first_row, TOK_DEV, 0).reshape(TOK_DEV, HEADS, HD)
        key_part = lax.dynamic_slice_in_dim(keys_padded, first_row, span, 0).reshape(span, HEADS, HD)
        value_part = lax.dynamic_slice_in_dim(values_padded, first_row, span, 0).reshape(span, HEADS, HD)
        allowed = (key_rel <= query_pos) & (key_rel > query_pos - WINDOW) & (first_row + key_rel >= 0)
        local_part = attend(query_part, key_part, value_part, allowed)
        routed_part = lax.dynamic_slice_in_dim(routed, first_row, TOK_DEV, 0).reshape(TOK_DEV, HEADS, HD)
        return (routed_part.astype(jnp.float32) + local_part).astype(jnp.bfloat16).reshape(TOK_DEV, width)

    attended = lax.map(one_shard, jnp.arange(N_SEQ, dtype=jnp.int32)).reshape(tokens_all, width)
    return jnp.dot(attended, out_weight, preferred_element_type=jnp.float32).astype(jnp.bfloat16)
```

```python
import jax
import jax.numpy as jnp
from jax import lax
from jax.experimental import pallas as pl
from jax.experimental.pallas import tpu as pltpu
from jax.sharding import Mesh
from jax.sharding import PartitionSpec as P

HD = 128
BLOCK = 8
WINDOW = 1024
SEQ = ("seq_0", "seq_1", "seq_2")
MESH = pl.DeviceIdType.MESH
TILE = 128
PIECE = 4 * TILE
ID_ROWS = 16
ROWS = PIECE + 2 * ID_ROWS
SUBS = 2
SUB = ROWS // SUBS
STEPS = 5
NEG = -1e30
F32 = jnp.float32
BF16 = jnp.bfloat16


def kernel(
    q_in, k_in, v_in, w_in, id_in, out_ref,
    q_buf, slots, o_buf, att, w_buf, part, parts_in, m_r, m_l, acc_r, acc_l, q_id,
    u_send, u_recv, ag_send, ag_recv, ret_send, ret_recv, rs_send, rs_recv, w_sem,
):
    z, y, c = (lax.axis_index(a) for a in SEQ)
    x = lax.axis_index("head")
    nz, nx = lax.axis_size("seq_0"), lax.axis_size("head")
    par = y % 2
    mate = y + 1 - 2 * par
    twin = 1 - c
    piece = 4 * z + 2 * par + c
    place = 2 * par + c
    head = y // 2
    z_up, z_down = (z + 1) % nz, (z + nz - 1) % nz
    dests = [(2 * i + y // 4, (y % 4) // 2) for i in range(4)]
    sources = [(4 * par + 2 * c + r // 2, r % 2 + 0 * c) for r in range(4)]

    def other(yy, cc):
        return jnp.logical_or(yy != y, cc != c)

    def remote(src, dst, send_sem, recv_sem, to):
        return pltpu.make_async_remote_copy(
            src_ref=src, dst_ref=dst, send_sem=send_sem, recv_sem=recv_sem,
            device_id=to, device_id_type=MESH,
        )

    here = (z, mate, c, x)

    def wait_recv(dst, sem):
        remote(dst, dst, sem, sem, here).wait_recv()

    def wait_send(src, sem):
        remote(src, src, sem, sem, here).wait_send()

    w_copy = pltpu.make_async_copy(w_in, w_buf, w_sem)
    w_copy.start()

    barrier = pltpu.get_barrier_semaphore()
    apart = jnp.int32(0)
    for yy, cc in dests + sources:
        far = other(yy, cc)
        apart = apart + far.astype(jnp.int32)

        @pl.when(far)
        def _():
            pl.semaphore_signal(barrier, 1, device_id=(z, yy, cc, x), device_id_type=MESH)

    near = [(z_up, y, c, x), (z_down, y, c, x), (z, mate, c, x), (z, y, twin, x)]
    near += [(z, y, c, (x + d) % nx) for d in range(1, 4)]
    for to in near:
        pl.semaphore_signal(barrier, 1, device_id=to, device_id_type=MESH)
    pl.semaphore_wait(barrier, apart + len(near))

    def landing(j, r):
        rows = pl.ds(pl.multiple_of(r * TILE, TILE), TILE)
        ids = pl.ds(pl.multiple_of(PIECE + ID_ROWS * (r // 2), ID_ROWS), ID_ROWS)
        lanes = pl.ds(pl.multiple_of(HD * (r % 2), HD), HD)
        return [
            slots.at[j, rows, 0:HD],
            slots.at[j, rows, HD : 2 * HD],
            slots.at[j, ids, lanes],
            q_buf.at[rows, :],
        ]

    for i, (yy, cc) in enumerate(dests):
        lanes = slice(i * HD, (i + 1) * HD)
        leaving = [k_in.at[:, lanes], v_in.at[:, lanes], id_in, q_in.at[:, lanes]]
        landed = landing(4 * z + 2 * (yy % 2) + cc, place)
        far = other(yy, cc)

        @pl.when(far)
        def _():
            for t in range(4):
                remote(
                    leaving[t], landed[t], u_send.at[i, t], u_recv.at[place, t], (z, yy, cc, x)
                ).start()

        @pl.when(jnp.logical_not(far))
        def _():
            for t in range(4):
                pltpu.make_async_copy(leaving[t], landed[t], u_recv.at[place, t]).start()

    m_r[...] = jnp.full_like(m_r, NEG)
    m_l[...] = jnp.full_like(m_l, NEG)
    acc_r[...] = jnp.zeros_like(acc_r)
    acc_l[...] = jnp.zeros_like(acc_l)

    def step_of(s, d):
        down = jnp.where(s <= 4, -s, -3), (s == 5)
        up = jnp.where(s <= 3, s, s - 3), (s >= 4)
        across = jnp.where(s <= 3, 1 - s, s - 1), (s >= 1)
        dz = jnp.where(d == 0, down[0], jnp.where(d == 1, up[0], across[0]))
        flip = jnp.where(d == 0, down[1], jnp.where(d == 1, up[1], across[1]))
        return dz, flip.astype(jnp.int32)

    def slot_of(dz, flip):
        return 4 * ((z + dz + nz) % nz) + 2 * (par + flip - 2 * par * flip) + c

    def sub_of(j, sub):
        return slots.at[j, pl.ds(sub * SUB, SUB), :]

    targets = [(z_up, y, c, x), (z_down, y, c, x), (z, mate, c, x)]

    def send_step(s, sub):
        for d, (shift, turn) in enumerate(((1, 0), (-1, 0), (0, 1))):
            dz, flip = step_of(s, d)
            j = slot_of(dz + shift, jnp.int32(0) if turn else flip)
            ref = sub_of(j, sub)
            remote(ref, ref, ag_send.at[d, s, sub], ag_recv.at[j, sub], targets[d]).start()

    def send_twin(j, d, s, sub):
        ref = sub_of(j, sub)
        remote(ref, ref, ag_send.at[3 + d, s, sub], ag_recv.at[j, sub], (z, y, twin, x)).start()

    for r in range(4):
        landed = landing(piece, r)
        for t in range(3):
            wait_recv(landed[t], u_recv.at[r, t])
    for sub in range(SUBS):
        send_step(jnp.int32(1), sub)
        send_twin(piece, 0, 0, sub)
    for r in range(4):
        wait_recv(landing(piece, r)[3], u_recv.at[r, 3])

    def ids_of(j):
        first = slots[j, PIECE : PIECE + ID_ROWS, :].astype(F32)[0:1, :]
        second = slots[j, PIECE + ID_ROWS : ROWS, :].astype(F32)[0:1, :]
        return jnp.concatenate([first, second], axis=1)

    own_ids = ids_of(piece)
    eye = lax.broadcasted_iota(jnp.int32, (TILE, TILE), 0) == lax.broadcasted_iota(
        jnp.int32, (TILE, TILE), 1
    )
    for r in range(4):
        row = jnp.broadcast_to(own_ids[:, r * TILE : (r + 1) * TILE], (TILE, TILE))
        column = jnp.sum(jnp.where(eye, row, 0.0), axis=1, keepdims=True)
        q_id[r * TILE : (r + 1) * TILE, :] = jnp.broadcast_to(column, (TILE, TILE))

    factor = HD ** -0.5 * 1.4426950408889634

    def across_keys(col):
        return jnp.concatenate([col] * 4, axis=1)

    def accumulate(scores, values, rows, m_ref, acc_ref):
        before = m_ref[rows, :]
        after = jnp.maximum(before, jnp.max(scores, axis=1, keepdims=True))
        weights = jnp.exp2(scores - across_keys(after))
        kept = jnp.exp2(before - after)
        m_ref[rows, :] = after
        acc_ref[rows, :] = acc_ref[rows, :] * jnp.concatenate([kept, kept], axis=1) + jnp.dot(
            weights.astype(BF16), values, preferred_element_type=F32
        )

    def attend(j, near_by):
        keys = slots[j, 0:PIECE, 0:HD]
        values = jnp.concatenate(
            [slots[j, 0:PIECE, HD : 2 * HD], jnp.ones((PIECE, HD), BF16)], axis=1
        )
        key_ids = ids_of(j)
        for r in range(4):
            rows = slice(r * TILE, (r + 1) * TILE)
            scores = lax.dot_general(
                q_buf[rows, :], keys, (((1,), (1,)), ((), ())), preferred_element_type=F32
            ) * factor
            same = across_keys(q_id[rows, :]) == key_ids
            if near_by:
                ahead = (
                    (j - piece) * PIECE - r * TILE
                    + lax.broadcasted_iota(jnp.int32, (TILE, PIECE), 1)
                    - lax.broadcasted_iota(jnp.int32, (TILE, PIECE), 0)
                )
                causal = ahead <= 0
                same = jnp.logical_and(same, causal)
                window = jnp.logical_and(causal, ahead > -WINDOW)
                accumulate(jnp.where(window, scores, NEG), values, rows, m_l, acc_l)
            accumulate(jnp.where(same, scores, NEG), values, rows, m_r, acc_r)

    def turn(t, carry):
        s = jnp.where(t < 2, 0, (t - 2) // 6 + 1)
        d6 = jnp.where(t < 2, 3 * t, (t - 2) % 6)
        d = d6 % 3
        from_twin = d6 // 3

        @pl.when(jnp.logical_and(t >= 2, d6 == 0))
        def _():
            for sub in range(SUBS):
                arrived = [slot_of(*step_of(s, e)) for e in range(3)]
                for e in range(3):
                    wait_recv(sub_of(arrived[e], sub), ag_recv.at[arrived[e], sub])

                @pl.when(s < STEPS)
                def _():
                    send_step(s + 1, sub)

                for e in range(3):
                    send_twin(arrived[e], e, s, sub)

        dz, flip = step_of(s, d)
        first = (s > 0).astype(jnp.int32)
        j = slot_of(dz * first, flip * first)
        j = j + from_twin * (1 - 2 * c)

        @pl.when(from_twin == 1)
        def _():
            for sub in range(SUBS):
                wait_recv(sub_of(j, sub), ag_recv.at[j, sub])

        back = piece - j

        @pl.when(jnp.logical_and(back >= 0, back <= 2))
        def _():
            attend(j, True)

        @pl.when(back > 2)
        def _():
            attend(j, False)

        return carry

    lax.fori_loop(0, 2 + 6 * STEPS, turn, 0)

    columns = pl.ds(pl.multiple_of(head * HD, HD), HD)
    for r, (yy, cc) in enumerate(sources):
        rows = slice(r * TILE, (r + 1) * TILE)
        routed = (acc_r[rows, 0:HD] / acc_r[rows, HD : 2 * HD]).astype(BF16).astype(F32)
        local = acc_l[rows, 0:HD] / acc_l[rows, HD : 2 * HD]
        o_buf[rows, :] = (routed + local).astype(BF16)
        far = other(yy, cc)

        @pl.when(far)
        def _():
            remote(
                o_buf.at[rows, :], att.at[:, columns], ret_send.at[r], ret_recv.at[head],
                (z, yy, cc, x),
            ).start()

        @pl.when(jnp.logical_not(far))
        def _():
            pltpu.make_async_copy(o_buf.at[rows, :], att.at[:, columns], ret_recv.at[head]).start()

    w_copy.wait()
    for i in range(4):
        wait_recv(att.at[:, i * HD : (i + 1) * HD], ret_recv.at[i])

    def partial(column_of):
        columns = pl.ds(pl.multiple_of(column_of * 4 * HD, 4 * HD), 4 * HD)
        return jnp.dot(att[...], w_buf[:, columns], preferred_element_type=F32)

    for d in (2, 1, 3):
        to = (x + d) % nx
        part[d - 1] = partial(to).astype(BF16)
        remote(
            part.at[d - 1], parts_in.at[d - 1], rs_send.at[d - 1], rs_recv.at[d - 1], (z, y, c, to)
        ).start()
    total = partial(x)
    for d in (1, 3, 2):
        wait_recv(parts_in.at[d - 1], rs_recv.at[d - 1])
        total = total + parts_in[d - 1].astype(F32)
    out_ref[...] = total.astype(BF16)

    for i, (yy, cc) in enumerate(dests):
        lanes = slice(i * HD, (i + 1) * HD)

        @pl.when(other(yy, cc))
        def _():
            for t, ref in enumerate((k_in.at[:, lanes], v_in.at[:, lanes], id_in, q_in.at[:, lanes])):
                wait_send(ref, u_send.at[i, t])

    for r, (yy, cc) in enumerate(sources):
        @pl.when(other(yy, cc))
        def _():
            wait_send(o_buf.at[r * TILE : (r + 1) * TILE, :], ret_send.at[r])

    for sub in range(SUBS):
        wait_send(sub_of(0, sub), ag_send.at[3, 0, sub])

    def settle(s, carry):
        for d in range(6):
            for sub in range(SUBS):
                wait_send(sub_of(0, sub), ag_send.at[d, s, sub])
        return carry

    lax.fori_loop(1, STEPS + 1, settle, 0)
    for d in range(3):
        wait_send(part.at[d], rs_send.at[d])


def body(query_rows, key_rows, value_rows, out_weight, cluster_ids):
    tokens, width = query_rows.shape
    ids = jnp.repeat(cluster_ids[0], BLOCK).astype(BF16)
    ids = jnp.broadcast_to(ids[None, :], (ID_ROWS, tokens))
    dma = pltpu.SemaphoreType.DMA
    return pl.pallas_call(
        kernel,
        out_shape=jax.ShapeDtypeStruct((tokens, width), BF16),
        in_specs=[pl.BlockSpec(memory_space=pl.ANY)] * 5,
        out_specs=pl.BlockSpec(memory_space=pltpu.VMEM),
        scratch_shapes=[
            pltpu.VMEM((PIECE, HD), BF16),
            pltpu.VMEM((32, ROWS, 2 * HD), BF16),
            pltpu.VMEM((PIECE, HD), BF16),
            pltpu.VMEM((tokens, width), BF16),
            pltpu.VMEM(out_weight.shape, BF16),
            pltpu.VMEM((3, tokens, width), BF16),
            pltpu.VMEM((3, tokens, width), BF16),
            pltpu.VMEM((PIECE, HD), F32),
            pltpu.VMEM((PIECE, HD), F32),
            pltpu.VMEM((PIECE, 2 * HD), F32),
            pltpu.VMEM((PIECE, 2 * HD), F32),
            pltpu.VMEM((PIECE, HD), F32),
            dma((4, 4)),
            dma((4, 4)),
            dma((6, STEPS + 1, SUBS)),
            dma((32, SUBS)),
            dma((4,)),
            dma((4,)),
            dma((3,)),
            dma((3,)),
            dma,
        ],
        compiler_params=pltpu.CompilerParams(collective_id=0, has_side_effects=True),
        name="attention",
    )(query_rows, key_rows, value_rows, out_weight, ids)


def solution(mesh):
    split = Mesh(
        mesh.devices.reshape(8, 8, 2, mesh.shape["head"]), ("seq_0", "seq_1", "seq_2", "head")
    )
    return jax.shard_map(
        body,
        mesh=split,
        in_specs=(P(SEQ, "head"), P(SEQ, "head"), P(SEQ, "head"), P("head", None), P(SEQ, None)),
        out_specs=P(SEQ, "head"),
        check_vma=False,
    )
```

```python
import jax
import jax.numpy as jnp
from jax import lax
from jax.experimental import pallas as pl
from jax.experimental.pallas import tpu as pltpu
from jax.sharding import Mesh
from jax.sharding import PartitionSpec as P

HD = 128
BLOCK = 8
WINDOW = 1024
SEQ = ("seq_0", "seq_1", "seq_2")
MESH = pl.DeviceIdType.MESH
TILE = 128
PIECE = 4 * TILE
SUBS = 4
STEPS = 5
NEG = -1e30
F32 = jnp.float32
BF16 = jnp.bfloat16


def kernel(
    q_in, k_in, v_in, w_in, id_in, out_ref,
    q_buf, slots, id_row, id_slots, o_buf, att, w_buf, part, relay_out, relay_in, parts_in,
    m_r, m_l, acc_r, acc_l, q_id,
    u_send, u_recv, ag_send, ag_recv, id_send, id_recv, ret_send, ret_recv, rs_send, rs_recv, w_sem,
):
    z, y, c = (lax.axis_index(a) for a in SEQ)
    x = lax.axis_index("head")
    nz, ny, nx = lax.axis_size("seq_0"), lax.axis_size("seq_1"), lax.axis_size("head")
    par = y % 2
    mate = y + 1 - 2 * par
    twin = 1 - c
    piece = 4 * z + 2 * c + par
    place = 2 * ((y // 2) % 2) + c
    head = y // 2
    z_up, z_down = (z + 1) % nz, (z + nz - 1) % nz
    x_up, x_down = (x + 1) % nx, (x + nx - 1) % nx
    dests = [(y + far) % ny for far in (3, ny - 3, 1, ny - 1)]
    sources = [(1 - par + 4 * c + 2 * (r // 2), r % 2) for r in range(4)]

    def remote(src, dst, send_sem, recv_sem, to):
        return pltpu.make_async_remote_copy(
            src_ref=src, dst_ref=dst, send_sem=send_sem, recv_sem=recv_sem,
            device_id=to, device_id_type=MESH,
        )

    here = (z, mate, c, x)

    def wait_recv(dst, sem):
        remote(dst, dst, sem, sem, here).wait_recv()

    def wait_send(src, sem):
        remote(src, src, sem, sem, here).wait_send()

    barrier = pltpu.get_barrier_semaphore()
    near = [(z, yy, y // 4, x) for yy in dests] + [(z, yy, cc, x) for yy, cc in sources]
    near += [(z_up, y, c, x), (z_down, y, c, x), (z, mate, c, x), (z, y, twin, x)]
    near += [(z, y, c, x_up), (z, y, c, x_down)]
    for to in near:
        pl.semaphore_signal(barrier, 1, device_id=to, device_id_type=MESH)

    w_copy = pltpu.make_async_copy(w_in, w_buf, w_sem)
    w_copy.start()
    block_of = lax.broadcasted_iota(jnp.int32, (1, TILE), 1) // BLOCK
    row = jnp.zeros((1, TILE), jnp.int32)
    for b in range(TILE // BLOCK):
        row = jnp.where(block_of == b, id_in[0, b], row)
    id_row[...] = row
    m_r[...] = jnp.full_like(m_r, NEG)
    m_l[...] = jnp.full_like(m_l, NEG)
    acc_r[...] = jnp.zeros_like(acc_r)
    acc_l[...] = jnp.zeros_like(acc_l)

    pl.semaphore_wait(barrier, len(near))

    def rows_of(r):
        return pl.ds(pl.multiple_of(r * TILE, TILE), TILE)

    def landing(j, r):
        return [
            slots.at[j, rows_of(r), 0:HD],
            slots.at[j, rows_of(r), HD : 2 * HD],
            id_slots.at[j, r],
            q_buf.at[rows_of(r), :],
        ]

    def leaving(yy):
        lanes = pl.ds(pl.multiple_of((yy // 2) * HD, HD), HD)
        return [k_in.at[:, lanes], v_in.at[:, lanes], id_row, q_in.at[:, lanes]]

    for tensors in ((0, 1, 2), (3,)):
        for i, yy in enumerate(dests):
            landed = landing(4 * z + 2 * (y // 4) + (1 - par), place)
            for t in tensors:
                remote(
                    leaving(yy)[t], landed[t], u_send.at[i, t], u_recv.at[place, t],
                    (z, yy, y // 4, x),
                ).start()

    def step_of(s, d):
        down = jnp.where(s <= 4, -s, -3), (s == 5)
        up = jnp.where(s <= 3, s, s - 3), (s >= 4)
        across = jnp.where(s <= 3, 1 - s, s - 1), (s >= 1)
        dz = jnp.where(d == 0, down[0], jnp.where(d == 1, up[0], across[0]))
        flip = jnp.where(d == 0, down[1], jnp.where(d == 1, up[1], across[1]))
        return dz, flip.astype(jnp.int32)

    def slot_of(dz, flip):
        return 4 * ((z + dz + nz) % nz) + 2 * c + par + flip - 2 * par * flip

    def sub_of(j, sub):
        return slots.at[j, rows_of(sub), :]

    targets = [(z_up, y, c, x), (z_down, y, c, x), (z, mate, c, x)]

    def send(j, d, s, sub, to):
        ref = sub_of(j, sub)
        remote(ref, ref, ag_send.at[d, s, sub], ag_recv.at[j, sub], to).start()

    def send_ids(j, d, s, to):
        remote(id_slots.at[j], id_slots.at[j], id_send.at[d, s], id_recv.at[j], to).start()

    def source_slots(s):
        found = []
        for d, (shift, turned) in enumerate(((1, 0), (-1, 0), (0, 1))):
            dz, flip = step_of(s, d)
            found.append(slot_of(dz + shift, jnp.int32(0) if turned else flip))
        return found

    for r in range(4):
        landed = landing(piece, r)
        for t in range(3):
            wait_recv(landed[t], u_recv.at[r, t])
        for d in range(3):
            send(piece, d, 1, r, targets[d])
        send(piece, 3, 0, r, (z, y, twin, x))
    for d in range(3):
        send_ids(piece, d, 1, targets[d])
    send_ids(piece, 3, 0, (z, y, twin, x))

    def ids_of(j):
        return jnp.concatenate([id_slots[j, r] for r in range(4)], axis=1).astype(F32)

    own_ids = ids_of(piece)
    eye = lax.broadcasted_iota(jnp.int32, (TILE, TILE), 0) == lax.broadcasted_iota(
        jnp.int32, (TILE, TILE), 1
    )
    for r in range(4):
        row = jnp.broadcast_to(own_ids[:, r * TILE : (r + 1) * TILE], (TILE, TILE))
        column = jnp.sum(jnp.where(eye, row, 0.0), axis=1, keepdims=True)
        q_id[r * TILE : (r + 1) * TILE, :] = jnp.broadcast_to(column, (TILE, TILE))
    for r in range(4):
        wait_recv(landing(piece, r)[3], u_recv.at[r, 3])

    factor = HD ** -0.5 * 1.4426950408889634

    def across_keys(col):
        return jnp.concatenate([col] * 4, axis=1)

    def accumulate(scores, values, rows, m_ref, acc_ref):
        before = m_ref[rows, :]
        after = jnp.maximum(before, jnp.max(scores, axis=1, keepdims=True))
        weights = jnp.exp2(scores - across_keys(after))
        kept = jnp.exp2(before - after)
        m_ref[rows, :] = after
        acc_ref[rows, :] = acc_ref[rows, :] * jnp.concatenate([kept, kept], axis=1) + jnp.dot(
            weights.astype(BF16), values, preferred_element_type=F32
        )

    def start_of(j):
        return 1024 * (j // 2) + 256 * (1 - j % 2)

    def attend(j, near_by):
        keys = slots[j, :, 0:HD]
        values = jnp.concatenate([slots[j, :, HD : 2 * HD], jnp.ones((PIECE, HD), BF16)], axis=1)
        key_ids = ids_of(j)
        for r in range(4):
            rows = slice(r * TILE, (r + 1) * TILE)
            scores = lax.dot_general(
                q_buf[rows, :], keys, (((1,), (1,)), ((), ())), preferred_element_type=F32
            ) * factor
            same = across_keys(q_id[rows, :]) == key_ids
            if near_by:
                lane = lax.broadcasted_iota(jnp.int32, (TILE, PIECE), 1)
                ahead = (
                    start_of(j) - start_of(piece) - r * TILE - 256 * (r // 2)
                    + lane + jnp.where(lane >= 256, 256, 0)
                    - lax.broadcasted_iota(jnp.int32, (TILE, PIECE), 0)
                )
                causal = ahead <= 0
                same = jnp.logical_and(same, causal)
                window = jnp.logical_and(causal, ahead > -WINDOW)
                accumulate(jnp.where(window, scores, NEG), values, rows, m_l, acc_l)
            accumulate(jnp.where(same, scores, NEG), values, rows, m_r, acc_r)

    def turn(t, carry):
        s, k = t // 6, t % 6
        d, from_twin = k % 3, k // 3
        dz, flip = step_of(s, d)
        later = (s > 0).astype(jnp.int32)
        j = slot_of(dz * later, flip * later) + from_twin * (2 - 4 * c)
        used = jnp.logical_or(s > 0, d == 0)

        @pl.when(jnp.logical_and(used, from_twin == 1))
        def _():
            wait_recv(id_slots.at[j], id_recv.at[j])
            for sub in range(SUBS):
                wait_recv(sub_of(j, sub), ag_recv.at[j, sub])

        back = piece // 2 - j // 2

        @pl.when(jnp.logical_and(used, jnp.logical_and(back >= 0, back <= 1)))
        def _():
            attend(j, True)

        @pl.when(jnp.logical_and(used, back > 1))
        def _():
            attend(j, False)

        @pl.when(jnp.logical_and(s < STEPS, d != 1))
        def _():
            sub = (2 * k) // 3
            arrived = [slot_of(*step_of(s + 1, e)) for e in range(3)]
            onward = source_slots(s + 2)
            for e in range(3):
                wait_recv(sub_of(arrived[e], sub), ag_recv.at[arrived[e], sub])

            @pl.when(s + 1 < STEPS)
            def _():
                for e in range(3):
                    send(onward[e], e, s + 2, sub, targets[e])

            for e in range(3):
                send(arrived[e], 3 + e, s + 1, sub, (z, y, twin, x))

            @pl.when(sub == 0)
            def _():
                for e in range(3):
                    wait_recv(id_slots.at[arrived[e]], id_recv.at[arrived[e]])

                @pl.when(s + 1 < STEPS)
                def _():
                    for e in range(3):
                        send_ids(onward[e], e, s + 2, targets[e])

                for e in range(3):
                    send_ids(arrived[e], 3 + e, s + 1, (z, y, twin, x))

        return carry

    lax.fori_loop(0, 6 * (STEPS + 1), turn, 0)

    columns = pl.ds(pl.multiple_of(head * HD, HD), HD)
    for r, (yy, cc) in enumerate(sources):
        rows = slice(r * TILE, (r + 1) * TILE)
        routed = (acc_r[rows, 0:HD] / acc_r[rows, HD : 2 * HD]).astype(BF16).astype(F32)
        local = acc_l[rows, 0:HD] / acc_l[rows, HD : 2 * HD]
        o_buf[rows, :] = (routed + local).astype(BF16)
        remote(
            o_buf.at[rows, :], att.at[:, columns], ret_send.at[r], ret_recv.at[head],
            (z, yy, cc, x),
        ).start()

    w_copy.wait()
    for i in range(4):
        wait_recv(att.at[:, i * HD : (i + 1) * HD], ret_recv.at[i])

    def partial(column_of):
        columns = pl.ds(pl.multiple_of(column_of * 4 * HD, 4 * HD), 4 * HD)
        return jnp.dot(att[...], w_buf[:, columns], preferred_element_type=F32)

    low, high = slice(0, TILE // 2), slice(TILE // 2, TILE)
    sides = ((x_up, low, high), (x_down, high, low))
    part[2] = partial((x + 2) % nx).astype(BF16)
    for e, (to, passed, _) in enumerate(sides):
        remote(
            part.at[2, passed, :], relay_in.at[e], rs_send.at[e, 0], rs_recv.at[e, 0], (z, y, c, to)
        ).start()
    sums = []
    for e, (to, passed, direct) in enumerate(sides):
        here_sum = partial(to)
        part[e] = here_sum.astype(BF16)
        remote(
            part.at[e, direct, :], parts_in.at[e, direct, :], rs_send.at[e, 1], rs_recv.at[e, 1],
            (z, y, c, to),
        ).start()
        sums.append(here_sum[passed, :])
    total = partial(x)
    for e, (to, passed, direct) in enumerate(sides):
        wait_recv(relay_in.at[e], rs_recv.at[e, 0])
        relay_out[e] = (sums[e] + relay_in[e].astype(F32)).astype(BF16)
        remote(
            relay_out.at[e], parts_in.at[e, passed, :], rs_send.at[e, 2], rs_recv.at[e, 2],
            (z, y, c, to),
        ).start()
    for e, (to, passed, direct) in enumerate(sides):
        wait_recv(parts_in.at[e, direct, :], rs_recv.at[e, 1])
    for e, (to, passed, direct) in enumerate(sides):
        wait_recv(parts_in.at[e, passed, :], rs_recv.at[e, 2])
    out_ref[...] = (total + parts_in[0].astype(F32) + parts_in[1].astype(F32)).astype(BF16)

    for i, yy in enumerate(dests):
        for t, ref in enumerate(leaving(yy)):
            wait_send(ref, u_send.at[i, t])
    for r in range(4):
        wait_send(o_buf.at[r * TILE : (r + 1) * TILE, :], ret_send.at[r])
    wait_send(id_slots.at[0], id_send.at[3, 0])
    for sub in range(SUBS):
        wait_send(sub_of(0, sub), ag_send.at[3, 0, sub])

    def settle(s, carry):
        for d in range(6):
            wait_send(id_slots.at[0], id_send.at[d, s])
            for sub in range(SUBS):
                wait_send(sub_of(0, sub), ag_send.at[d, s, sub])
        return carry

    lax.fori_loop(1, STEPS + 1, settle, 0)
    for e in range(2):
        for n in range(3):
            wait_send(relay_out.at[e], rs_send.at[e, n])


def body(query_rows, key_rows, value_rows, out_weight, cluster_ids):
    tokens, width = query_rows.shape
    dma = pltpu.SemaphoreType.DMA
    anywhere = pl.BlockSpec(memory_space=pl.ANY)
    return pl.pallas_call(
        kernel,
        out_shape=jax.ShapeDtypeStruct((tokens, width), BF16),
        in_specs=[anywhere] * 4 + [pl.BlockSpec(memory_space=pltpu.SMEM)],
        out_specs=pl.BlockSpec(memory_space=pltpu.VMEM),
        scratch_shapes=[
            pltpu.VMEM((PIECE, HD), BF16),
            pltpu.VMEM((32, PIECE, 2 * HD), BF16),
            pltpu.VMEM((1, TILE), jnp.int32),
            pltpu.VMEM((32, 4, 1, TILE), jnp.int32),
            pltpu.VMEM((PIECE, HD), BF16),
            pltpu.VMEM((tokens, width), BF16),
            pltpu.VMEM(out_weight.shape, BF16),
            pltpu.VMEM((3, tokens, width), BF16),
            pltpu.VMEM((2, tokens // 2, width), BF16),
            pltpu.VMEM((2, tokens // 2, width), BF16),
            pltpu.VMEM((2, tokens, width), BF16),
            pltpu.VMEM((PIECE, HD), F32),
            pltpu.VMEM((PIECE, HD), F32),
            pltpu.VMEM((PIECE, 2 * HD), F32),
            pltpu.VMEM((PIECE, 2 * HD), F32),
            pltpu.VMEM((PIECE, HD), F32),
            dma((4, 4)),
            dma((4, 4)),
            dma((6, STEPS + 1, SUBS)),
            dma((32, SUBS)),
            dma((6, STEPS + 1)),
            dma((32,)),
            dma((4,)),
            dma((4,)),
            dma((2, 3)),
            dma((2, 3)),
            dma,
        ],
        compiler_params=pltpu.CompilerParams(collective_id=0, has_side_effects=True),
        name="attention",
    )(query_rows, key_rows, value_rows, out_weight, cluster_ids)


def solution(mesh):
    split = Mesh(
        mesh.devices.reshape(8, 8, 2, mesh.shape["head"]), ("seq_0", "seq_1", "seq_2", "head")
    )
    return jax.shard_map(
        body,
        mesh=split,
        in_specs=(P(SEQ, "head"), P(SEQ, "head"), P(SEQ, "head"), P("head", None), P(SEQ, None)),
        out_specs=P(SEQ, "head"),
        check_vma=False,
    )
```

```python
import jax
import jax.numpy as jnp
from jax import lax
from jax.experimental import pallas as pl
from jax.experimental.pallas import tpu as pltpu
from jax.sharding import Mesh
from jax.sharding import PartitionSpec as P

HD = 128
BLOCK = 8
WINDOW = 1024
SEQ = ("seq_0", "seq_1", "seq_2")
MESH = pl.DeviceIdType.MESH
TILE = 128
PIECE = 4 * TILE
SUBS = 4
STEPS = 4
NEG = -1e30
F32 = jnp.float32
BF16 = jnp.bfloat16


def kernel(
    q_in, k_in, v_in, w_in, id_in, out_ref,
    q_buf, slots, id_row, id_slots, o_buf, o_away, o_in, stats, stats_in, att, w_buf,
    part, relay_out, relay_in, parts_in, m_r, m_l, acc_r, acc_l, q_id,
    u_send, u_recv, ag_send, ag_recv, id_send, id_recv, y_send, q_recv, o_send, o_recv,
    ret_send, ret_recv, rs_send, rs_recv, w_sem,
):
    z, y, c = (lax.axis_index(a) for a in SEQ)
    x = lax.axis_index("head")
    nz, ny, nx = lax.axis_size("seq_0"), lax.axis_size("seq_1"), lax.axis_size("head")
    par = y % 2
    mate = y + 1 - 2 * par
    twin = 1 - c
    piece = 4 * z + 2 * c + par
    place = 2 * ((y // 2) % 2) + c
    head = y // 2
    z_up, z_down = (z + 1) % nz, (z + nz - 1) % nz
    x_up, x_down = (x + 1) % nx, (x + nx - 1) % nx
    dests = [(y + far) % ny for far in (3, ny - 3, 1, ny - 1)]
    sources = [(1 - par + 4 * c + 2 * (r // 2), r % 2) for r in range(4)]

    def remote(src, dst, send_sem, recv_sem, to):
        return pltpu.make_async_remote_copy(
            src_ref=src, dst_ref=dst, send_sem=send_sem, recv_sem=recv_sem,
            device_id=to, device_id_type=MESH,
        )

    here = (z, mate, c, x)

    def wait_recv(dst, sem):
        remote(dst, dst, sem, sem, here).wait_recv()

    def wait_send(src, sem):
        remote(src, src, sem, sem, here).wait_send()

    barrier = pltpu.get_barrier_semaphore()
    near = [(z, yy, y // 4, x) for yy in dests] + [(z, yy, cc, x) for yy, cc in sources]
    near += [(z_up, y, c, x), (z_down, y, c, x), (z, mate, c, x), (z, y, twin, x)]
    near += [(z, y, c, x_up), (z, y, c, x_down)]
    for to in near:
        pl.semaphore_signal(barrier, 1, device_id=to, device_id_type=MESH)

    w_copy = pltpu.make_async_copy(w_in, w_buf, w_sem)
    w_copy.start()
    block_of = lax.broadcasted_iota(jnp.int32, (1, TILE), 1) // BLOCK
    row = jnp.zeros((1, TILE), jnp.int32)
    for b in range(TILE // BLOCK):
        row = jnp.where(block_of == b, id_in[0, b], row)
    id_row[...] = row
    m_r[...] = jnp.full_like(m_r, NEG)
    m_l[...] = jnp.full_like(m_l, NEG)
    acc_r[...] = jnp.zeros_like(acc_r)
    acc_l[...] = jnp.zeros_like(acc_l)

    pl.semaphore_wait(barrier, len(near))

    def rows_of(r):
        return pl.ds(pl.multiple_of(r * TILE, TILE), TILE)

    def landing(j, r):
        return [
            slots.at[j, rows_of(r), 0:HD],
            slots.at[j, rows_of(r), HD : 2 * HD],
            id_slots.at[j, r],
            q_buf.at[rows_of(r), :],
        ]

    def leaving(yy):
        lanes = pl.ds(pl.multiple_of((yy // 2) * HD, HD), HD)
        return [k_in.at[:, lanes], v_in.at[:, lanes], id_row, q_in.at[:, lanes]]

    for tensors in ((0, 1, 2), (3,)):
        for i, yy in enumerate(dests):
            landed = landing(4 * z + 2 * (y // 4) + (1 - par), place)
            for t in tensors:
                remote(
                    leaving(yy)[t], landed[t], u_send.at[i, t], u_recv.at[place, t],
                    (z, yy, y // 4, x),
                ).start()

    def slot_of(dz, core, p):
        return 4 * ((z + dz + nz) % nz) + 2 * core + p

    def sub_of(j, sub):
        return slots.at[j, rows_of(sub), :]

    to_up, to_down, to_mate, to_twin = (z_up, y, c, x), (z_down, y, c, x), here, (z, y, twin, x)

    def send(j, sub, send_sem, to):
        ref = sub_of(j, sub)
        remote(ref, ref, send_sem, ag_recv.at[j, sub], to).start()

    def send_ids(j, send_sem, to):
        remote(id_slots.at[j], id_slots.at[j], send_sem, id_recv.at[j], to).start()

    def send_whole(j, n, to):
        send_ids(j, y_send.at[n, SUBS], to)
        for sub in range(SUBS):
            send(j, sub, y_send.at[n, sub], to)

    def wait_whole(j):
        wait_recv(id_slots.at[j], id_recv.at[j])
        for sub in range(SUBS):
            wait_recv(sub_of(j, sub), ag_recv.at[j, sub])

    for r in range(4):
        landed = landing(piece, r)
        for t in range(3):
            wait_recv(landed[t], u_recv.at[r, t])
        send(piece, r, ag_send.at[0, 1, r], to_up)
        send(piece, r, ag_send.at[1, 1, r], to_down)
        send(piece, r, ag_send.at[2, 0, r], to_twin)
    send_ids(piece, id_send.at[0, 1], to_up)
    send_ids(piece, id_send.at[1, 1], to_down)
    send_ids(piece, id_send.at[2, 0], to_twin)

    own_q, mate_q = q_buf.at[0:PIECE, :], q_buf.at[PIECE : 2 * PIECE, :]
    for r in range(4):
        wait_recv(landing(piece, r)[3], u_recv.at[r, 3])
    remote(own_q, mate_q, y_send.at[0, 0], q_recv, to_mate).start()
    send_whole(piece, 1, to_mate)

    def ids_of(j):
        return jnp.concatenate([id_slots[j, r] for r in range(4)], axis=1).astype(F32)

    eye = lax.broadcasted_iota(jnp.int32, (TILE, TILE), 0) == lax.broadcasted_iota(
        jnp.int32, (TILE, TILE), 1
    )

    def column_from(row):
        column = jnp.sum(
            jnp.where(eye, jnp.broadcast_to(row, (TILE, TILE)), 0.0), axis=1, keepdims=True
        )
        return jnp.broadcast_to(column, (TILE, TILE))

    def row_from(column):
        return jnp.sum(jnp.where(eye, column, 0.0), axis=0, keepdims=True)

    def set_query_ids(first, j):
        found = ids_of(j)
        for r in range(4):
            q_id[first + r * TILE : first + (r + 1) * TILE, :] = column_from(
                found[:, r * TILE : (r + 1) * TILE]
            )

    set_query_ids(0, piece)

    factor = HD ** -0.5 * 1.4426950408889634

    def across_keys(col):
        return jnp.concatenate([col] * 4, axis=1)

    def accumulate(scores, values, rows, m_ref, acc_ref):
        before = m_ref[rows, :]
        after = jnp.maximum(before, jnp.max(scores, axis=1, keepdims=True))
        weights = jnp.exp2(scores - across_keys(after))
        kept = jnp.exp2(before - after)
        m_ref[rows, :] = after
        acc_ref[rows, :] = acc_ref[rows, :] * jnp.concatenate([kept, kept], axis=1) + jnp.dot(
            weights.astype(BF16), values, preferred_element_type=F32
        )

    def start_of(j):
        return 1024 * (j // 2) + 256 * (1 - j % 2)

    def attend(j, near_by):
        keys = slots[j, :, 0:HD]
        values = jnp.concatenate([slots[j, :, HD : 2 * HD], jnp.ones((PIECE, HD), BF16)], axis=1)
        key_ids = ids_of(j)
        for r in range(4 if near_by else 8):
            rows = slice(r * TILE, (r + 1) * TILE)
            scores = lax.dot_general(
                q_buf[rows, :], keys, (((1,), (1,)), ((), ())), preferred_element_type=F32
            ) * factor
            same = across_keys(q_id[rows, :]) == key_ids
            if near_by:
                lane = lax.broadcasted_iota(jnp.int32, (TILE, PIECE), 1)
                ahead = (
                    start_of(j) - start_of(piece) - r * TILE - 256 * (r // 2)
                    + lane + jnp.where(lane >= 256, 256, 0)
                    - lax.broadcasted_iota(jnp.int32, (TILE, PIECE), 0)
                )
                causal = ahead <= 0
                same = jnp.logical_and(same, causal)
                window = jnp.logical_and(causal, ahead > -WINDOW)
                accumulate(jnp.where(window, scores, NEG), values, rows, m_l, acc_l)
            accumulate(jnp.where(same, scores, NEG), values, rows, m_r, acc_r)

    mate_piece = slot_of(0, c, 1 - par)
    before_mate = 2 * ((piece // 2 + 2 * nz - 1) % (2 * nz)) + 1 - par

    def turn(t, carry):
        s, k = t // 5, t % 5
        extra = k == 2
        from_twin = (k > 2).astype(jnp.int32)
        upward = (k == 1) | (k == 4)
        core = c + from_twin * (1 - 2 * c)
        j = slot_of(jnp.where(upward, s, -s), core, par)
        j = jnp.where(extra, jnp.where(s == 2, mate_piece, before_mate), j)
        used = jnp.where(extra, (s == 2) | (s == 3), jnp.logical_not(upward) | ((s > 0) & (s < 4)))

        @pl.when((t == 5))
        def _():
            wait_recv(mate_q, q_recv)
            wait_recv(id_slots.at[mate_piece], id_recv.at[mate_piece])
            set_query_ids(PIECE, mate_piece)

        @pl.when(used & (from_twin == 1))
        def _():
            wait_whole(j)

        @pl.when((s == 1) & (k == 3) & (c == 0))
        def _():
            send_whole(j, 2, to_mate)

        @pl.when(extra & (s == 2))
        def _():
            for sub in range(SUBS):
                wait_recv(sub_of(j, sub), ag_recv.at[j, sub])

            @pl.when(c == 0)
            def _():
                send_whole(j, 3, to_twin)

        @pl.when(extra & (s == 3))
        def _():
            wait_whole(j)

        back = piece // 2 - j // 2

        @pl.when(used & (back >= 0) & (back <= 1))
        def _():
            attend(j, True)

        @pl.when(used & (back > 1))
        def _():
            attend(j, False)

        @pl.when((s < STEPS) & jnp.logical_not(extra))
        def _():
            sub = k - (k > 2).astype(jnp.int32)
            n = s + 1
            low, high = slot_of(-n, c, par), slot_of(n, c, par)
            lower, upper = sub < 2, sub >= 2

            @pl.when((n < STEPS) | lower)
            def _():
                wait_recv(sub_of(low, sub), ag_recv.at[low, sub])

                @pl.when((n + 1 < STEPS) | ((n + 1 == STEPS) & lower))
                def _():
                    send(low, sub, ag_send.at[0, n + 1, sub], to_up)

                send(low, sub, ag_send.at[2, n, sub], to_twin)

            @pl.when((n < STEPS) | upper)
            def _():
                wait_recv(sub_of(high, sub), ag_recv.at[high, sub])

                @pl.when((n + 1 < STEPS) | ((n + 1 == STEPS) & upper))
                def _():
                    send(high, sub, ag_send.at[1, n + 1, sub], to_down)

                send(high, sub, ag_send.at[3, n, sub], to_twin)

            @pl.when(sub == 0)
            def _():
                wait_recv(id_slots.at[low], id_recv.at[low])
                send_ids(low, id_send.at[2, n], to_twin)

                @pl.when(n < STEPS)
                def _():
                    wait_recv(id_slots.at[high], id_recv.at[high])
                    send_ids(low, id_send.at[0, n + 1], to_up)
                    send_ids(high, id_send.at[3, n], to_twin)

                    @pl.when(n + 1 < STEPS)
                    def _():
                        send_ids(high, id_send.at[1, n + 1], to_down)

        return carry

    lax.fori_loop(0, 5 * (STEPS + 1), turn, 0)

    for r in range(4):
        rows = slice(PIECE + r * TILE, PIECE + (r + 1) * TILE)
        stats[2 * r : 2 * r + 1, :] = row_from(m_r[rows, :])
        stats[2 * r + 1 : 2 * r + 2, :] = row_from(acc_r[rows, HD : 2 * HD])
    remote(stats, stats_in, o_send.at[4], o_recv.at[4], to_mate).start()
    for r in range(4):
        rows = slice(PIECE + r * TILE, PIECE + (r + 1) * TILE)
        here_rows = slice(r * TILE, (r + 1) * TILE)
        weight = jnp.maximum(acc_r[rows, HD : 2 * HD], 1e-30)
        o_away[here_rows, :] = (acc_r[rows, 0:HD] / weight).astype(BF16)
        remote(
            o_away.at[here_rows, :], o_in.at[here_rows, :], o_send.at[r], o_recv.at[r], to_mate
        ).start()
    wait_recv(stats_in, o_recv.at[4])

    columns = pl.ds(pl.multiple_of(head * HD, HD), HD)
    for r, (yy, cc) in enumerate(sources):
        rows = slice(r * TILE, (r + 1) * TILE)
        wait_recv(o_in.at[rows, :], o_recv.at[r])
        m_here, m_there = m_r[rows, :], column_from(stats_in[2 * r : 2 * r + 1, :])
        largest = jnp.maximum(m_here, m_there)
        kept = jnp.exp2(m_here - largest)
        added = jnp.exp2(m_there - largest) * column_from(stats_in[2 * r + 1 : 2 * r + 2, :])
        routed = (acc_r[rows, 0:HD] * kept + o_in[rows, :].astype(F32) * added) / (
            acc_r[rows, HD : 2 * HD] * kept + added
        )
        routed = routed.astype(BF16).astype(F32)
        local = acc_l[rows, 0:HD] / acc_l[rows, HD : 2 * HD]
        o_buf[rows, :] = (routed + local).astype(BF16)
        remote(
            o_buf.at[rows, :], att.at[:, columns], ret_send.at[r], ret_recv.at[head],
            (z, yy, cc, x),
        ).start()

    w_copy.wait()
    for i in range(4):
        wait_recv(att.at[:, i * HD : (i + 1) * HD], ret_recv.at[i])

    def partial(column_of):
        columns = pl.ds(pl.multiple_of(column_of * 4 * HD, 4 * HD), 4 * HD)
        return jnp.dot(att[...], w_buf[:, columns], preferred_element_type=F32)

    low, high = slice(0, TILE // 2), slice(TILE // 2, TILE)
    sides = ((x_up, low, high), (x_down, high, low))
    part[2] = partial((x + 2) % nx).astype(BF16)
    for e, (to, passed, _) in enumerate(sides):
        remote(
            part.at[2, passed, :], relay_in.at[e], rs_send.at[e, 0], rs_recv.at[e, 0], (z, y, c, to)
        ).start()
    sums = []
    for e, (to, passed, direct) in enumerate(sides):
        here_sum = partial(to)
        part[e] = here_sum.astype(BF16)
        remote(
            part.at[e, direct, :], parts_in.at[e, direct, :], rs_send.at[e, 1], rs_recv.at[e, 1],
            (z, y, c, to),
        ).start()
        sums.append(here_sum[passed, :])
    total = partial(x)
    for e, (to, passed, direct) in enumerate(sides):
        wait_recv(relay_in.at[e], rs_recv.at[e, 0])
        relay_out[e] = (sums[e] + relay_in[e].astype(F32)).astype(BF16)
        remote(
            relay_out.at[e], parts_in.at[e, passed, :], rs_send.at[e, 2], rs_recv.at[e, 2],
            (z, y, c, to),
        ).start()
    for e, (to, passed, direct) in enumerate(sides):
        wait_recv(parts_in.at[e, direct, :], rs_recv.at[e, 1])
    for e, (to, passed, direct) in enumerate(sides):
        wait_recv(parts_in.at[e, passed, :], rs_recv.at[e, 2])
    out_ref[...] = (total + parts_in[0].astype(F32) + parts_in[1].astype(F32)).astype(BF16)

    for i, yy in enumerate(dests):
        for t, ref in enumerate(leaving(yy)):
            wait_send(ref, u_send.at[i, t])
    for r in range(4):
        wait_send(o_buf.at[r * TILE : (r + 1) * TILE, :], ret_send.at[r])
    for r in range(4):
        wait_send(o_away.at[r * TILE : (r + 1) * TILE, :], o_send.at[r])
    wait_send(stats, o_send.at[4])
    wait_send(own_q, y_send.at[0, 0])

    def sent_whole(n):
        for sub in range(SUBS):
            wait_send(sub_of(0, sub), y_send.at[n, sub])
        wait_send(id_slots.at[0], y_send.at[n, SUBS])

    sent_whole(1)

    @pl.when(c == 0)
    def _():
        sent_whole(2)
        sent_whole(3)

    wait_send(id_slots.at[0], id_send.at[2, 0])
    for sub in range(SUBS):
        wait_send(sub_of(0, sub), ag_send.at[2, 0, sub])

    def settle(s, carry):
        for d in range(4):
            wait_send(id_slots.at[0], id_send.at[d, s])
            for sub in range(SUBS):
                wait_send(sub_of(0, sub), ag_send.at[d, s, sub])
        return carry

    lax.fori_loop(1, STEPS, settle, 0)
    for d in (0, 2):
        wait_send(id_slots.at[0], id_send.at[d, STEPS])
    for d in range(4):
        for sub in range(2):
            n = sub + 2 * (d % 2)
            wait_send(sub_of(0, n), ag_send.at[d, STEPS, n])
    for e in range(2):
        for n in range(3):
            wait_send(relay_out.at[e], rs_send.at[e, n])


def body(query_rows, key_rows, value_rows, out_weight, cluster_ids):
    tokens, width = query_rows.shape
    dma = pltpu.SemaphoreType.DMA
    anywhere = pl.BlockSpec(memory_space=pl.ANY)
    return pl.pallas_call(
        kernel,
        out_shape=jax.ShapeDtypeStruct((tokens, width), BF16),
        in_specs=[anywhere] * 4 + [pl.BlockSpec(memory_space=pltpu.SMEM)],
        out_specs=pl.BlockSpec(memory_space=pltpu.VMEM),
        scratch_shapes=[
            pltpu.VMEM((2 * PIECE, HD), BF16),
            pltpu.VMEM((32, PIECE, 2 * HD), BF16),
            pltpu.VMEM((1, TILE), jnp.int32),
            pltpu.VMEM((32, 4, 1, TILE), jnp.int32),
            pltpu.VMEM((PIECE, HD), BF16),
            pltpu.VMEM((PIECE, HD), BF16),
            pltpu.VMEM((PIECE, HD), BF16),
            pltpu.VMEM((8, TILE), F32),
            pltpu.VMEM((8, TILE), F32),
            pltpu.VMEM((tokens, width), BF16),
            pltpu.VMEM(out_weight.shape, BF16),
            pltpu.VMEM((3, tokens, width), BF16),
            pltpu.VMEM((2, tokens // 2, width), BF16),
            pltpu.VMEM((2, tokens // 2, width), BF16),
            pltpu.VMEM((2, tokens, width), BF16),
            pltpu.VMEM((2 * PIECE, HD), F32),
            pltpu.VMEM((PIECE, HD), F32),
            pltpu.VMEM((2 * PIECE, 2 * HD), F32),
            pltpu.VMEM((PIECE, 2 * HD), F32),
            pltpu.VMEM((2 * PIECE, HD), F32),
            dma((4, 4)),
            dma((4, 4)),
            dma((4, STEPS + 1, SUBS)),
            dma((32, SUBS)),
            dma((4, STEPS + 1)),
            dma((32,)),
            dma((4, SUBS + 1)),
            dma,
            dma((5,)),
            dma((5,)),
            dma((4,)),
            dma((4,)),
            dma((2, 3)),
            dma((2, 3)),
            dma,
        ],
        compiler_params=pltpu.CompilerParams(collective_id=0, has_side_effects=True),
        name="attention",
    )(query_rows, key_rows, value_rows, out_weight, cluster_ids)


def solution(mesh):
    split = Mesh(
        mesh.devices.reshape(8, 8, 2, mesh.shape["head"]), ("seq_0", "seq_1", "seq_2", "head")
    )
    return jax.shard_map(
        body,
        mesh=split,
        in_specs=(P(SEQ, "head"), P(SEQ, "head"), P(SEQ, "head"), P("head", None), P(SEQ, None)),
        out_specs=P(SEQ, "head"),
        check_vma=False,
    )
```

```python
import jax
import jax.numpy as jnp
from jax import lax
from jax.experimental import pallas as pl
from jax.experimental.pallas import tpu as pltpu
from jax.sharding import Mesh
from jax.sharding import PartitionSpec as P

HD = 128
BLOCK = 8
WINDOW = 1024
SEQ = ("seq_0", "seq_1", "seq_2")
MESH = pl.DeviceIdType.MESH
TILE = 128
PIECE = 4 * TILE
SUBS = 4
STEPS = 4
NEG = -1e30
F32 = jnp.float32
BF16 = jnp.bfloat16


def kernel(
    q_in, k_in, v_in, w_in, id_in, out_ref,
    q_buf, slots, id_row, id_slots, o_buf, o_away, o_in, stats, stats_in, att, w_buf,
    m_r, m_l, acc_r, acc_l, q_id,
    u_send, u_recv, ag_send, ag_recv, id_send, id_recv, y_send, q_recv, o_send, o_recv,
    ret_send, ret_recv, x_send, x_recv, w_send, w_recv,
):
    z, y, c = (lax.axis_index(a) for a in SEQ)
    x = lax.axis_index("head")
    nz, ny, nx = lax.axis_size("seq_0"), lax.axis_size("seq_1"), lax.axis_size("head")
    par = y % 2
    mate = y + 1 - 2 * par
    twin = 1 - c
    piece = 4 * z + 2 * c + par
    place = 2 * ((y // 2) % 2) + c
    head = y // 2
    z_up, z_down = (z + 1) % nz, (z + nz - 1) % nz
    x_up, x_down, x_far = (x + 1) % nx, (x + nx - 1) % nx, (x + 2) % nx
    dests = [(y + far) % ny for far in (1, ny - 1, 3, ny - 3)]
    first = 2 * ((1 - par + 4 * c - y + 2 * ny) % ny == 5).astype(jnp.int32)
    sources = [(1 - par + 4 * c + 2 * (r // 2), r % 2) for r in range(4)]

    def remote(src, dst, send_sem, recv_sem, to):
        return pltpu.make_async_remote_copy(
            src_ref=src, dst_ref=dst, send_sem=send_sem, recv_sem=recv_sem,
            device_id=to, device_id_type=MESH,
        )

    here = (z, mate, c, x)

    def wait_recv(dst, sem):
        remote(dst, dst, sem, sem, here).wait_recv()

    def wait_send(src, sem):
        remote(src, src, sem, sem, here).wait_send()

    barrier = pltpu.get_barrier_semaphore()
    near = [(z, yy, y // 4, x) for yy in dests] + [(z, yy, cc, x) for yy, cc in sources]
    near += [(z_up, y, c, x), (z_down, y, c, x), (z, mate, c, x), (z, y, twin, x)]
    near += [(z, y, c, x_up), (z, y, c, x_down), (z, y, c, x_far)]
    for to in near:
        pl.semaphore_signal(barrier, 1, device_id=to, device_id_type=MESH)

    def w_columns(to):
        return w_in.at[:, pl.ds(pl.multiple_of(to * 4 * HD, 4 * HD), 4 * HD)]

    pltpu.make_async_copy(w_columns(x), w_buf.at[x], w_recv.at[0]).start()
    block_of = lax.broadcasted_iota(jnp.int32, (1, TILE), 1) // BLOCK
    row = jnp.zeros((1, TILE), jnp.int32)
    for b in range(TILE // BLOCK):
        row = jnp.where(block_of == b, id_in[0, b], row)
    id_row[...] = row
    m_r[...] = jnp.full_like(m_r, NEG)
    m_l[...] = jnp.full_like(m_l, NEG)
    acc_r[...] = jnp.zeros_like(acc_r)
    acc_l[...] = jnp.zeros_like(acc_l)

    pl.semaphore_wait(barrier, len(near))

    def rows_of(r):
        return pl.ds(pl.multiple_of(r * TILE, TILE), TILE)

    def landing(j, r):
        return [
            slots.at[j, rows_of(r), 0:HD],
            slots.at[j, rows_of(r), HD : 2 * HD],
            id_slots.at[j, r],
            q_buf.at[rows_of(r), :],
        ]

    def leaving(yy):
        lanes = pl.ds(pl.multiple_of((yy // 2) * HD, HD), HD)
        return [k_in.at[:, lanes], v_in.at[:, lanes], id_row, q_in.at[:, lanes]]

    for tensors in ((0, 1, 2), (3,)):
        for i, yy in enumerate(dests):
            landed = landing(4 * z + 2 * (y // 4) + (1 - par), place)
            for t in tensors:
                remote(
                    leaving(yy)[t], landed[t], u_send.at[i, t], u_recv.at[place, t],
                    (z, yy, y // 4, x),
                ).start()

    for d, to in enumerate((x_up, x_down, x_far)):
        remote(
            w_columns(to), w_buf.at[x], w_send.at[d], w_recv.at[1 + d], (z, y, c, to)
        ).start()

    def slot_of(dz, core, p):
        return 4 * ((z + dz + nz) % nz) + 2 * core + p

    def sub_of(j, sub):
        return slots.at[j, rows_of(sub), :]

    to_up, to_down, to_mate, to_twin = (z_up, y, c, x), (z_down, y, c, x), here, (z, y, twin, x)

    def send(j, sub, send_sem, to):
        ref = sub_of(j, sub)
        remote(ref, ref, send_sem, ag_recv.at[j, sub], to).start()

    def send_ids(j, send_sem, to):
        remote(id_slots.at[j], id_slots.at[j], send_sem, id_recv.at[j], to).start()

    def send_whole(j, n, to):
        send_ids(j, y_send.at[n, SUBS], to)
        for sub in range(SUBS):
            send(j, sub, y_send.at[n, sub], to)

    def wait_whole(j):
        wait_recv(id_slots.at[j], id_recv.at[j])
        for sub in range(SUBS):
            wait_recv(sub_of(j, sub), ag_recv.at[j, sub])

    for n in range(4):
        r = (first + n) % 4
        landed = landing(piece, r)
        for t in range(3):
            wait_recv(landed[t], u_recv.at[r, t])
        send(piece, r, ag_send.at[0, 1, r], to_up)
        send(piece, r, ag_send.at[1, 1, r], to_down)
        send(piece, r, ag_send.at[2, 0, r], to_twin)
    send_ids(piece, id_send.at[0, 1], to_up)
    send_ids(piece, id_send.at[1, 1], to_down)
    send_ids(piece, id_send.at[2, 0], to_twin)

    own_q, mate_q = q_buf.at[0:PIECE, :], q_buf.at[PIECE : 2 * PIECE, :]
    for r in range(4):
        wait_recv(landing(piece, r)[3], u_recv.at[r, 3])
    remote(own_q, mate_q, y_send.at[0, 0], q_recv, to_mate).start()
    send_whole(piece, 1, to_mate)

    def ids_of(j):
        return jnp.concatenate([id_slots[j, r] for r in range(4)], axis=1).astype(F32)

    eye = lax.broadcasted_iota(jnp.int32, (TILE, TILE), 0) == lax.broadcasted_iota(
        jnp.int32, (TILE, TILE), 1
    )

    def column_from(row):
        column = jnp.sum(
            jnp.where(eye, jnp.broadcast_to(row, (TILE, TILE)), 0.0), axis=1, keepdims=True
        )
        return jnp.broadcast_to(column, (TILE, TILE))

    def row_from(column):
        return jnp.sum(jnp.where(eye, column, 0.0), axis=0, keepdims=True)

    def set_query_ids(first, j):
        found = ids_of(j)
        for r in range(4):
            q_id[first + r * TILE : first + (r + 1) * TILE, :] = column_from(
                found[:, r * TILE : (r + 1) * TILE]
            )

    set_query_ids(0, piece)

    factor = HD ** -0.5 * 1.4426950408889634

    def across_keys(col):
        return jnp.concatenate([col] * 4, axis=1)

    def accumulate(scores, values, rows, m_ref, acc_ref):
        before = m_ref[rows, :]
        after = jnp.maximum(before, jnp.max(scores, axis=1, keepdims=True))
        weights = jnp.exp2(scores - across_keys(after))
        kept = jnp.exp2(before - after)
        m_ref[rows, :] = after
        acc_ref[rows, :] = acc_ref[rows, :] * jnp.concatenate([kept, kept], axis=1) + jnp.dot(
            weights.astype(BF16), values, preferred_element_type=F32
        )

    def start_of(j):
        return 1024 * (j // 2) + 256 * (1 - j % 2)

    def attend(j, near_by):
        keys = slots[j, :, 0:HD]
        values = jnp.concatenate([slots[j, :, HD : 2 * HD], jnp.ones((PIECE, HD), BF16)], axis=1)
        key_ids = ids_of(j)
        for r in range(4 if near_by else 8):
            rows = slice(r * TILE, (r + 1) * TILE)
            scores = lax.dot_general(
                q_buf[rows, :], keys, (((1,), (1,)), ((), ())), preferred_element_type=F32
            ) * factor
            same = across_keys(q_id[rows, :]) == key_ids
            if near_by:
                lane = lax.broadcasted_iota(jnp.int32, (TILE, PIECE), 1)
                ahead = (
                    start_of(j) - start_of(piece) - r * TILE - 256 * (r // 2)
                    + lane + jnp.where(lane >= 256, 256, 0)
                    - lax.broadcasted_iota(jnp.int32, (TILE, PIECE), 0)
                )
                causal = ahead <= 0
                same = jnp.logical_and(same, causal)
                window = jnp.logical_and(causal, ahead > -WINDOW)
                accumulate(jnp.where(window, scores, NEG), values, rows, m_l, acc_l)
            accumulate(jnp.where(same, scores, NEG), values, rows, m_r, acc_r)

    mate_piece = slot_of(0, c, 1 - par)
    before_mate = 2 * ((piece // 2 + 2 * nz - 1) % (2 * nz)) + 1 - par

    def turn(t, carry):
        s, k = t // 5, t % 5
        extra = k == 2
        from_twin = (k > 2).astype(jnp.int32)
        upward = (k == 1) | (k == 4)
        core = c + from_twin * (1 - 2 * c)
        j = slot_of(jnp.where(upward, s, -s), core, par)
        j = jnp.where(extra, jnp.where(s == 2, mate_piece, before_mate), j)
        used = jnp.where(extra, (s == 2) | (s == 3), jnp.logical_not(upward) | ((s > 0) & (s < 4)))

        @pl.when((t == 5))
        def _():
            wait_recv(mate_q, q_recv)
            wait_recv(id_slots.at[mate_piece], id_recv.at[mate_piece])
            set_query_ids(PIECE, mate_piece)

        @pl.when(used & (from_twin == 1))
        def _():
            wait_whole(j)

        @pl.when((s == 1) & (k == 3) & (c == 0))
        def _():
            send_whole(j, 2, to_mate)

        @pl.when(extra & (s == 2))
        def _():
            for sub in range(SUBS):
                wait_recv(sub_of(j, sub), ag_recv.at[j, sub])

            @pl.when(c == 0)
            def _():
                send_whole(j, 3, to_twin)

        @pl.when(extra & (s == 3))
        def _():
            wait_whole(j)

        back = piece // 2 - j // 2

        @pl.when(used & (back >= 0) & (back <= 1))
        def _():
            attend(j, True)

        @pl.when(used & (back > 1))
        def _():
            attend(j, False)

        @pl.when((s < STEPS) & jnp.logical_not(extra))
        def _():
            order = k - (k > 2).astype(jnp.int32)
            sub = (first + order) % 4
            n = s + 1
            low, high = slot_of(-n, c, par), slot_of(n, c, par)
            lower, upper = sub < 2, sub >= 2

            @pl.when((n < STEPS) | lower)
            def _():
                wait_recv(sub_of(low, sub), ag_recv.at[low, sub])

                @pl.when((n + 1 < STEPS) | ((n + 1 == STEPS) & lower))
                def _():
                    send(low, sub, ag_send.at[0, n + 1, sub], to_up)

                send(low, sub, ag_send.at[2, n, sub], to_twin)

            @pl.when((n < STEPS) | upper)
            def _():
                wait_recv(sub_of(high, sub), ag_recv.at[high, sub])

                @pl.when((n + 1 < STEPS) | ((n + 1 == STEPS) & upper))
                def _():
                    send(high, sub, ag_send.at[1, n + 1, sub], to_down)

                send(high, sub, ag_send.at[3, n, sub], to_twin)

            @pl.when(order == 0)
            def _():
                wait_recv(id_slots.at[low], id_recv.at[low])
                send_ids(low, id_send.at[2, n], to_twin)

                @pl.when(n < STEPS)
                def _():
                    wait_recv(id_slots.at[high], id_recv.at[high])
                    send_ids(low, id_send.at[0, n + 1], to_up)
                    send_ids(high, id_send.at[3, n], to_twin)

                    @pl.when(n + 1 < STEPS)
                    def _():
                        send_ids(high, id_send.at[1, n + 1], to_down)

        return carry

    lax.fori_loop(0, 5 * (STEPS + 1), turn, 0)

    for r in range(4):
        rows = slice(PIECE + r * TILE, PIECE + (r + 1) * TILE)
        stats[2 * r : 2 * r + 1, :] = row_from(m_r[rows, :])
        stats[2 * r + 1 : 2 * r + 2, :] = row_from(acc_r[rows, HD : 2 * HD])
    remote(stats, stats_in, o_send.at[4], o_recv.at[4], to_mate).start()
    for r in range(4):
        rows = slice(PIECE + r * TILE, PIECE + (r + 1) * TILE)
        here_rows = slice(r * TILE, (r + 1) * TILE)
        weight = jnp.maximum(acc_r[rows, HD : 2 * HD], 1e-30)
        o_away[here_rows, :] = (acc_r[rows, 0:HD] / weight).astype(BF16)
        remote(
            o_away.at[here_rows, :], o_in.at[here_rows, :], o_send.at[r], o_recv.at[r], to_mate
        ).start()
    wait_recv(stats_in, o_recv.at[4])

    columns = pl.ds(pl.multiple_of(head * HD, HD), HD)
    for r, (yy, cc) in enumerate(sources):
        rows = slice(r * TILE, (r + 1) * TILE)
        wait_recv(o_in.at[rows, :], o_recv.at[r])
        m_here, m_there = m_r[rows, :], column_from(stats_in[2 * r : 2 * r + 1, :])
        largest = jnp.maximum(m_here, m_there)
        kept = jnp.exp2(m_here - largest)
        added = jnp.exp2(m_there - largest) * column_from(stats_in[2 * r + 1 : 2 * r + 2, :])
        routed = (acc_r[rows, 0:HD] * kept + o_in[rows, :].astype(F32) * added) / (
            acc_r[rows, HD : 2 * HD] * kept + added
        )
        routed = routed.astype(BF16).astype(F32)
        local = acc_l[rows, 0:HD] / acc_l[rows, HD : 2 * HD]
        o_buf[rows, :] = (routed + local).astype(BF16)
        remote(
            o_buf.at[rows, :], att.at[x, :, columns], ret_send.at[r], ret_recv.at[head],
            (z, yy, cc, x),
        ).start()

    def block(plane, n):
        lanes = pl.ds(pl.multiple_of((dests[n] // 2) * HD, HD), HD)
        return att.at[plane, :, lanes]

    def pass_on(plane, n, way, slot, to):
        ref = block(plane, n)
        remote(ref, ref, x_send.at[way, n], x_recv.at[slot, n], (z, y, c, to)).start()

    def project(plane):
        return jnp.dot(att[plane], w_buf[plane], preferred_element_type=F32)

    for n in range(4):
        wait_recv(block(x, n), ret_recv.at[dests[n] // 2])
        pass_on(x, n, 0, 0, x_up)
        pass_on(x, n, 1, 1, x_down)
    for d, plane in enumerate((x, x_down, x_up, x_far)):
        wait_recv(w_buf.at[plane], w_recv.at[d])
    total = project(x)
    for n in range(4):
        if n % 2 == 0:
            wait_recv(block(x_down, n), x_recv.at[0, n])
            pass_on(x_down, n, 2, 2, x_up)
        else:
            wait_recv(block(x_up, n), x_recv.at[1, n])
            pass_on(x_up, n, 2, 2, x_down)
    for n in (1, 3):
        wait_recv(block(x_down, n), x_recv.at[0, n])
    total = total + project(x_down)
    for n in (0, 2):
        wait_recv(block(x_up, n), x_recv.at[1, n])
    total = total + project(x_up)
    for n in range(4):
        wait_recv(block(x_far, n), x_recv.at[2, n])
    out_ref[...] = total + project(x_far)

    for i, yy in enumerate(dests):
        for t, ref in enumerate(leaving(yy)):
            wait_send(ref, u_send.at[i, t])
    for r in range(4):
        wait_send(o_buf.at[r * TILE : (r + 1) * TILE, :], ret_send.at[r])
    for r in range(4):
        wait_send(o_away.at[r * TILE : (r + 1) * TILE, :], o_send.at[r])
    wait_send(stats, o_send.at[4])
    wait_send(own_q, y_send.at[0, 0])

    def sent_whole(n):
        for sub in range(SUBS):
            wait_send(sub_of(0, sub), y_send.at[n, sub])
        wait_send(id_slots.at[0], y_send.at[n, SUBS])

    sent_whole(1)

    @pl.when(c == 0)
    def _():
        sent_whole(2)
        sent_whole(3)

    wait_send(id_slots.at[0], id_send.at[2, 0])
    for sub in range(SUBS):
        wait_send(sub_of(0, sub), ag_send.at[2, 0, sub])

    def settle(s, carry):
        for d in range(4):
            wait_send(id_slots.at[0], id_send.at[d, s])
            for sub in range(SUBS):
                wait_send(sub_of(0, sub), ag_send.at[d, s, sub])
        return carry

    lax.fori_loop(1, STEPS, settle, 0)
    for d in (0, 2):
        wait_send(id_slots.at[0], id_send.at[d, STEPS])
    for d in range(4):
        for sub in range(2):
            n = sub + 2 * (d % 2)
            wait_send(sub_of(0, n), ag_send.at[d, STEPS, n])
    for d in range(3):
        wait_send(w_buf.at[0], w_send.at[d])
        for n in range(4):
            wait_send(block(0, n), x_send.at[d, n])


def body(query_rows, key_rows, value_rows, out_weight, cluster_ids):
    tokens, width = query_rows.shape
    dma = pltpu.SemaphoreType.DMA
    anywhere = pl.BlockSpec(memory_space=pl.ANY)
    total = pl.pallas_call(
        kernel,
        out_shape=jax.ShapeDtypeStruct((tokens, width), F32),
        in_specs=[anywhere] * 4 + [pl.BlockSpec(memory_space=pltpu.SMEM)],
        out_specs=pl.BlockSpec(memory_space=pltpu.VMEM),
        scratch_shapes=[
            pltpu.VMEM((2 * PIECE, HD), BF16),
            pltpu.VMEM((32, PIECE, 2 * HD), BF16),
            pltpu.VMEM((1, TILE), jnp.int32),
            pltpu.VMEM((32, 4, 1, TILE), jnp.int32),
            pltpu.VMEM((PIECE, HD), BF16),
            pltpu.VMEM((PIECE, HD), BF16),
            pltpu.VMEM((PIECE, HD), BF16),
            pltpu.VMEM((8, TILE), F32),
            pltpu.VMEM((8, TILE), F32),
            pltpu.VMEM((4, tokens, width), BF16),
            pltpu.VMEM((4, width, width), BF16),
            pltpu.VMEM((2 * PIECE, HD), F32),
            pltpu.VMEM((PIECE, HD), F32),
            pltpu.VMEM((2 * PIECE, 2 * HD), F32),
            pltpu.VMEM((PIECE, 2 * HD), F32),
            pltpu.VMEM((2 * PIECE, HD), F32),
            dma((4, 4)),
            dma((4, 4)),
            dma((4, STEPS + 1, SUBS)),
            dma((32, SUBS)),
            dma((4, STEPS + 1)),
            dma((32,)),
            dma((4, SUBS + 1)),
            dma,
            dma((5,)),
            dma((5,)),
            dma((4,)),
            dma((4,)),
            dma((3, 4)),
            dma((3, 4)),
            dma((3,)),
            dma((4,)),
        ],
        compiler_params=pltpu.CompilerParams(collective_id=0, has_side_effects=True),
        name="attention",
    )(query_rows, key_rows, value_rows, out_weight, cluster_ids)
    return total.astype(BF16)


def solution(mesh):
    split = Mesh(
        mesh.devices.reshape(8, 8, 2, mesh.shape["head"]), ("seq_0", "seq_1", "seq_2", "head")
    )
    return jax.shard_map(
        body,
        mesh=split,
        in_specs=(P(SEQ, "head"), P(SEQ, "head"), P(SEQ, "head"), P("head", None), P(SEQ, None)),
        out_specs=P(SEQ, "head"),
        check_vma=False,
    )
```

```python
import jax
import jax.numpy as jnp
from jax import lax
from jax.experimental import pallas as pl
from jax.experimental.pallas import tpu as pltpu
from jax.sharding import Mesh
from jax.sharding import PartitionSpec as P

HD = 128
BLOCK = 8
WINDOW = 1024
SEQ = ("seq_0", "seq_1", "seq_2")
MESH = pl.DeviceIdType.MESH
TILE = 128
PIECE = 4 * TILE
SUBS = 4
STEPS = 4
NEG = -1e30
F32 = jnp.float32
BF16 = jnp.bfloat16


def kernel(
    q_in, k_in, v_in, w_in, id_in, out_ref,
    q_buf, slots, id_row, id_slots, o_buf, o_away, o_in, stats, stats_in, att, w_buf,
    m_r, m_l, acc_r, acc_l, q_id,
    u_send, u_recv, ag_send, ag_recv, id_send, id_recv, y_send, q_recv, o_send, o_recv,
    ret_send, ret_recv, x_send, x_recv, w_send, w_recv,
):
    z, y, c = (lax.axis_index(a) for a in SEQ)
    x = lax.axis_index("head")
    nz, ny, nx = lax.axis_size("seq_0"), lax.axis_size("seq_1"), lax.axis_size("head")
    par = y % 2
    mate = y + 1 - 2 * par
    twin = 1 - c
    piece = 4 * z + 2 * c + par
    place = 2 * ((y // 2) % 2) + c
    head = y // 2
    z_up, z_down = (z + 1) % nz, (z + nz - 1) % nz
    x_up, x_down, x_far = (x + 1) % nx, (x + nx - 1) % nx, (x + 2) % nx
    dests = [(y + far) % ny for far in (1, ny - 1, 3, ny - 3)]
    first = 2 * ((1 - par + 4 * c - y + 2 * ny) % ny == 5).astype(jnp.int32)
    sources = [(1 - par + 4 * c + 2 * (r // 2), r % 2) for r in range(4)]

    def remote(src, dst, send_sem, recv_sem, to):
        return pltpu.make_async_remote_copy(
            src_ref=src, dst_ref=dst, send_sem=send_sem, recv_sem=recv_sem,
            device_id=to, device_id_type=MESH,
        )

    here = (z, mate, c, x)

    def wait_recv(dst, sem):
        remote(dst, dst, sem, sem, here).wait_recv()

    def wait_send(src, sem):
        remote(src, src, sem, sem, here).wait_send()

    barrier = pltpu.get_barrier_semaphore()
    near = [(z, yy, y // 4, x) for yy in dests] + [(z, yy, cc, x) for yy, cc in sources]
    near += [(z_up, y, c, x), (z_down, y, c, x), (z, mate, c, x), (z, y, twin, x)]
    near += [(z, y, c, x_up), (z, y, c, x_down), (z, y, c, x_far)]
    for to in near:
        pl.semaphore_signal(barrier, 1, device_id=to, device_id_type=MESH)

    def w_columns(to):
        return w_in.at[:, pl.ds(pl.multiple_of(to * 4 * HD, 4 * HD), 4 * HD)]

    pltpu.make_async_copy(w_columns(x), w_buf.at[x], w_recv.at[0]).start()
    block_of = lax.broadcasted_iota(jnp.int32, (1, TILE), 1) // BLOCK
    row = jnp.zeros((1, TILE), jnp.int32)
    for b in range(TILE // BLOCK):
        row = jnp.where(block_of == b, id_in[0, b], row)
    id_row[...] = row
    m_r[...] = jnp.full_like(m_r, NEG)
    m_l[...] = jnp.full_like(m_l, NEG)
    acc_r[...] = jnp.zeros_like(acc_r)
    acc_l[...] = jnp.zeros_like(acc_l)

    pl.semaphore_wait(barrier, len(near))

    def rows_of(r):
        return pl.ds(pl.multiple_of(r * TILE, TILE), TILE)

    def landing(j, r):
        return [
            slots.at[j, rows_of(r), 0:HD],
            slots.at[j, rows_of(r), HD : 2 * HD],
            id_slots.at[j, r],
            q_buf.at[rows_of(r), :],
        ]

    def leaving(yy):
        lanes = pl.ds(pl.multiple_of((yy // 2) * HD, HD), HD)
        return [k_in.at[:, lanes], v_in.at[:, lanes], id_row, q_in.at[:, lanes]]

    for tensors in ((0, 1, 2), (3,)):
        for i, yy in enumerate(dests):
            landed = landing(4 * z + 2 * (y // 4) + (1 - par), place)
            for t in tensors:
                remote(
                    leaving(yy)[t], landed[t], u_send.at[i, t], u_recv.at[place, t],
                    (z, yy, y // 4, x),
                ).start()

    for d, to in enumerate((x_up, x_down, x_far)):
        remote(
            w_columns(to), w_buf.at[x], w_send.at[d], w_recv.at[1 + d], (z, y, c, to)
        ).start()

    def slot_of(dz, core, p):
        return 4 * ((z + dz + nz) % nz) + 2 * core + p

    def sub_of(j, sub):
        return slots.at[j, rows_of(sub), :]

    to_up, to_down, to_mate, to_twin = (z_up, y, c, x), (z_down, y, c, x), here, (z, y, twin, x)

    def send(j, sub, send_sem, to):
        ref = sub_of(j, sub)
        remote(ref, ref, send_sem, ag_recv.at[j, sub], to).start()

    def send_ids(j, send_sem, to):
        remote(id_slots.at[j], id_slots.at[j], send_sem, id_recv.at[j], to).start()

    def send_whole(j, n, to):
        send_ids(j, y_send.at[n, SUBS], to)
        for sub in range(SUBS):
            send(j, sub, y_send.at[n, sub], to)

    def wait_whole(j):
        wait_recv(id_slots.at[j], id_recv.at[j])
        for sub in range(SUBS):
            wait_recv(sub_of(j, sub), ag_recv.at[j, sub])

    for n in range(4):
        r = (first + n) % 4
        landed = landing(piece, r)
        for t in range(3):
            wait_recv(landed[t], u_recv.at[r, t])
        send(piece, r, ag_send.at[0, 1, r], to_up)
        send(piece, r, ag_send.at[1, 1, r], to_down)
        send(piece, r, ag_send.at[2, 0, r], to_twin)
    send_ids(piece, id_send.at[0, 1], to_up)
    send_ids(piece, id_send.at[1, 1], to_down)
    send_ids(piece, id_send.at[2, 0], to_twin)

    def forward(n, order):
        sub = (first + order) % 4
        low, high = slot_of(-n, c, par), slot_of(n, c, par)
        lower, upper = sub < 2, sub >= 2

        @pl.when((n < STEPS) | lower)
        def _():
            wait_recv(sub_of(low, sub), ag_recv.at[low, sub])

            @pl.when((n + 1 < STEPS) | ((n + 1 == STEPS) & lower))
            def _():
                send(low, sub, ag_send.at[0, n + 1, sub], to_up)

            send(low, sub, ag_send.at[2, n, sub], to_twin)

        @pl.when((n < STEPS) | upper)
        def _():
            wait_recv(sub_of(high, sub), ag_recv.at[high, sub])

            @pl.when((n + 1 < STEPS) | ((n + 1 == STEPS) & upper))
            def _():
                send(high, sub, ag_send.at[1, n + 1, sub], to_down)

            send(high, sub, ag_send.at[3, n, sub], to_twin)

        @pl.when(order == 0)
        def _():
            wait_recv(id_slots.at[low], id_recv.at[low])
            send_ids(low, id_send.at[2, n], to_twin)

            @pl.when(n < STEPS)
            def _():
                wait_recv(id_slots.at[high], id_recv.at[high])
                send_ids(low, id_send.at[0, n + 1], to_up)
                send_ids(high, id_send.at[3, n], to_twin)

                @pl.when(n + 1 < STEPS)
                def _():
                    send_ids(high, id_send.at[1, n + 1], to_down)

    def forward_first(order, carry):
        forward(jnp.int32(1), order)
        return carry

    lax.fori_loop(0, 2, forward_first, 0)

    own_q, mate_q = q_buf.at[0:PIECE, :], q_buf.at[PIECE : 2 * PIECE, :]
    for r in range(4):
        wait_recv(landing(piece, r)[3], u_recv.at[r, 3])
    remote(own_q, mate_q, y_send.at[0, 0], q_recv, to_mate).start()
    send_whole(piece, 1, to_mate)

    def ids_of(j):
        return jnp.concatenate([id_slots[j, r] for r in range(4)], axis=1).astype(F32)

    eye = lax.broadcasted_iota(jnp.int32, (TILE, TILE), 0) == lax.broadcasted_iota(
        jnp.int32, (TILE, TILE), 1
    )

    def column_from(row):
        column = jnp.sum(
            jnp.where(eye, jnp.broadcast_to(row, (TILE, TILE)), 0.0), axis=1, keepdims=True
        )
        return jnp.broadcast_to(column, (TILE, TILE))

    def row_from(column):
        return jnp.sum(jnp.where(eye, column, 0.0), axis=0, keepdims=True)

    def set_query_ids(first, j):
        found = ids_of(j)
        for r in range(4):
            q_id[first + r * TILE : first + (r + 1) * TILE, :] = column_from(
                found[:, r * TILE : (r + 1) * TILE]
            )

    set_query_ids(0, piece)

    factor = HD ** -0.5 * 1.4426950408889634

    def across_keys(col):
        return jnp.concatenate([col] * 4, axis=1)

    def accumulate(scores, values, rows, m_ref, acc_ref):
        before = m_ref[rows, :]
        after = jnp.maximum(before, jnp.max(scores, axis=1, keepdims=True))
        weights = jnp.exp2(scores - across_keys(after))
        kept = jnp.exp2(before - after)
        m_ref[rows, :] = after
        acc_ref[rows, :] = acc_ref[rows, :] * jnp.concatenate([kept, kept], axis=1) + jnp.dot(
            weights.astype(BF16), values, preferred_element_type=F32
        )

    def start_of(j):
        return 1024 * (j // 2) + 256 * (1 - j % 2)

    def attend(j, base, near_by):
        keys = slots[j, :, 0:HD]
        values = jnp.concatenate([slots[j, :, HD : 2 * HD], jnp.ones((PIECE, HD), BF16)], axis=1)
        key_ids = ids_of(j)
        for r in range(4):
            rows = slice(base + r * TILE, base + (r + 1) * TILE)
            scores = lax.dot_general(
                q_buf[rows, :], keys, (((1,), (1,)), ((), ())), preferred_element_type=F32
            ) * factor
            same = across_keys(q_id[rows, :]) == key_ids
            if near_by:
                lane = lax.broadcasted_iota(jnp.int32, (TILE, PIECE), 1)
                ahead = (
                    start_of(j) - start_of(piece) - r * TILE - 256 * (r // 2)
                    + lane + jnp.where(lane >= 256, 256, 0)
                    - lax.broadcasted_iota(jnp.int32, (TILE, PIECE), 0)
                )
                causal = ahead <= 0
                same = jnp.logical_and(same, causal)
                window = jnp.logical_and(causal, ahead > -WINDOW)
                accumulate(jnp.where(window, scores, NEG), values, rows, m_l, acc_l)
            accumulate(jnp.where(same, scores, NEG), values, rows, m_r, acc_r)

    mate_piece = slot_of(0, c, 1 - par)
    before_mate = 2 * ((piece // 2 + 2 * nz - 1) % (2 * nz)) + 1 - par

    def turn(t, carry):
        s, k = t // 5, t % 5
        extra = k == 2
        order = jnp.where(s == 0, k + 2, k - (k > 2).astype(jnp.int32))
        moves = jnp.where(s == 0, k < 2, (s < STEPS) & (k != 2))
        from_twin = (k > 2).astype(jnp.int32)
        upward = (k == 1) | (k == 4)
        core = c + from_twin * (1 - 2 * c)
        j = slot_of(jnp.where(upward, s, -s), core, par)
        j = jnp.where(extra, jnp.where(s == 2, mate_piece, before_mate), j)
        used = jnp.where(extra, (s == 2) | (s == 3), jnp.logical_not(upward) | ((s > 0) & (s < 4)))

        @pl.when((s == 1) & moves)
        def _():
            forward(s + 1, order)

        @pl.when(t == 5)
        def _():
            wait_recv(mate_q, q_recv)
            wait_recv(id_slots.at[mate_piece], id_recv.at[mate_piece])
            set_query_ids(PIECE, mate_piece)

        @pl.when(used & (from_twin == 1))
        def _():
            wait_whole(j)

        @pl.when((s == 1) & (k == 3) & (c == 0))
        def _():
            send_whole(j, 2, to_mate)

        @pl.when(extra & (s == 2))
        def _():
            for sub in range(SUBS):
                wait_recv(sub_of(j, sub), ag_recv.at[j, sub])

            @pl.when(c == 0)
            def _():
                send_whole(j, 3, to_twin)

        @pl.when(extra & (s == 3))
        def _():
            wait_whole(j)

        back = piece // 2 - j // 2

        @pl.when(used & (back >= 0) & (back <= 1))
        def _():
            attend(j, 0, True)

        @pl.when(used & (back > 1))
        def _():
            attend(j, PIECE, False)
            attend(j, 0, False)

        @pl.when((s != 1) & moves)
        def _():
            forward(s + 1, order)

        return carry

    lax.fori_loop(0, 5 * STEPS, turn, 0)

    last_own, last_twin = slot_of(STEPS, c, par), slot_of(STEPS, twin, par)

    def attend_far(j, base):
        @pl.when(piece // 2 - j // 2 > 1)
        def _():
            attend(j, base, False)

    attend_far(last_own, PIECE)
    attend_far(last_own, 0)
    wait_whole(last_twin)
    attend_far(last_twin, PIECE)

    for r in range(4):
        rows = slice(PIECE + r * TILE, PIECE + (r + 1) * TILE)
        stats[2 * r : 2 * r + 1, :] = row_from(m_r[rows, :])
        stats[2 * r + 1 : 2 * r + 2, :] = row_from(acc_r[rows, HD : 2 * HD])
    remote(stats, stats_in, o_send.at[4], o_recv.at[4], to_mate).start()
    for r in range(4):
        rows = slice(PIECE + r * TILE, PIECE + (r + 1) * TILE)
        here_rows = slice(r * TILE, (r + 1) * TILE)
        weight = jnp.maximum(acc_r[rows, HD : 2 * HD], 1e-30)
        o_away[here_rows, :] = (acc_r[rows, 0:HD] / weight).astype(BF16)
        remote(
            o_away.at[here_rows, :], o_in.at[here_rows, :], o_send.at[r], o_recv.at[r], to_mate
        ).start()
    attend_far(last_twin, 0)
    wait_recv(stats_in, o_recv.at[4])

    columns = pl.ds(pl.multiple_of(head * HD, HD), HD)
    for r, (yy, cc) in enumerate(sources):
        rows = slice(r * TILE, (r + 1) * TILE)
        wait_recv(o_in.at[rows, :], o_recv.at[r])
        m_here, m_there = m_r[rows, :], column_from(stats_in[2 * r : 2 * r + 1, :])
        largest = jnp.maximum(m_here, m_there)
        kept = jnp.exp2(m_here - largest)
        added = jnp.exp2(m_there - largest) * column_from(stats_in[2 * r + 1 : 2 * r + 2, :])
        routed = (acc_r[rows, 0:HD] * kept + o_in[rows, :].astype(F32) * added) / (
            acc_r[rows, HD : 2 * HD] * kept + added
        )
        routed = routed.astype(BF16).astype(F32)
        local = acc_l[rows, 0:HD] / acc_l[rows, HD : 2 * HD]
        o_buf[rows, :] = (routed + local).astype(BF16)
        remote(
            o_buf.at[rows, :], att.at[x, :, columns], ret_send.at[r], ret_recv.at[head],
            (z, yy, cc, x),
        ).start()

    def block(plane, n):
        lanes = pl.ds(pl.multiple_of((dests[n] // 2) * HD, HD), HD)
        return att.at[plane, :, lanes]

    def pass_on(plane, n, way, slot, to):
        ref = block(plane, n)
        remote(ref, ref, x_send.at[way, n], x_recv.at[slot, n], (z, y, c, to)).start()

    def project(plane):
        return jnp.dot(att[plane], w_buf[plane], preferred_element_type=F32)

    for n in range(4):
        wait_recv(block(x, n), ret_recv.at[dests[n] // 2])
        pass_on(x, n, 0, 0, x_up)
        pass_on(x, n, 1, 1, x_down)
    for d, plane in enumerate((x, x_down, x_up, x_far)):
        wait_recv(w_buf.at[plane], w_recv.at[d])
    total = project(x)
    for n in range(4):
        if n % 2 == 0:
            wait_recv(block(x_down, n), x_recv.at[0, n])
            pass_on(x_down, n, 2, 2, x_up)
        else:
            wait_recv(block(x_up, n), x_recv.at[1, n])
            pass_on(x_up, n, 2, 2, x_down)
    for n in (1, 3):
        wait_recv(block(x_down, n), x_recv.at[0, n])
    total = total + project(x_down)
    for n in (0, 2):
        wait_recv(block(x_up, n), x_recv.at[1, n])
    total = total + project(x_up)
    for n in range(4):
        wait_recv(block(x_far, n), x_recv.at[2, n])
    out_ref[...] = total + project(x_far)

    for i, yy in enumerate(dests):
        for t, ref in enumerate(leaving(yy)):
            wait_send(ref, u_send.at[i, t])
    for r in range(4):
        wait_send(o_buf.at[r * TILE : (r + 1) * TILE, :], ret_send.at[r])
    for r in range(4):
        wait_send(o_away.at[r * TILE : (r + 1) * TILE, :], o_send.at[r])
    wait_send(stats, o_send.at[4])
    wait_send(own_q, y_send.at[0, 0])

    def sent_whole(n):
        for sub in range(SUBS):
            wait_send(sub_of(0, sub), y_send.at[n, sub])
        wait_send(id_slots.at[0], y_send.at[n, SUBS])

    sent_whole(1)

    @pl.when(c == 0)
    def _():
        sent_whole(2)
        sent_whole(3)

    wait_send(id_slots.at[0], id_send.at[2, 0])
    for sub in range(SUBS):
        wait_send(sub_of(0, sub), ag_send.at[2, 0, sub])

    def settle(s, carry):
        for d in range(4):
            wait_send(id_slots.at[0], id_send.at[d, s])
            for sub in range(SUBS):
                wait_send(sub_of(0, sub), ag_send.at[d, s, sub])
        return carry

    lax.fori_loop(1, STEPS, settle, 0)
    for d in (0, 2):
        wait_send(id_slots.at[0], id_send.at[d, STEPS])
    for d in range(4):
        for sub in range(2):
            n = sub + 2 * (d % 2)
            wait_send(sub_of(0, n), ag_send.at[d, STEPS, n])
    for d in range(3):
        wait_send(w_buf.at[0], w_send.at[d])
        for n in range(4):
            wait_send(block(0, n), x_send.at[d, n])


def body(query_rows, key_rows, value_rows, out_weight, cluster_ids):
    tokens, width = query_rows.shape
    dma = pltpu.SemaphoreType.DMA
    anywhere = pl.BlockSpec(memory_space=pl.ANY)
    total = pl.pallas_call(
        kernel,
        out_shape=jax.ShapeDtypeStruct((tokens, width), F32),
        in_specs=[anywhere] * 4 + [pl.BlockSpec(memory_space=pltpu.SMEM)],
        out_specs=pl.BlockSpec(memory_space=pltpu.VMEM),
        scratch_shapes=[
            pltpu.VMEM((2 * PIECE, HD), BF16),
            pltpu.VMEM((32, PIECE, 2 * HD), BF16),
            pltpu.VMEM((1, TILE), jnp.int32),
            pltpu.VMEM((32, 4, 1, TILE), jnp.int32),
            pltpu.VMEM((PIECE, HD), BF16),
            pltpu.VMEM((PIECE, HD), BF16),
            pltpu.VMEM((PIECE, HD), BF16),
            pltpu.VMEM((8, TILE), F32),
            pltpu.VMEM((8, TILE), F32),
            pltpu.VMEM((4, tokens, width), BF16),
            pltpu.VMEM((4, width, width), BF16),
            pltpu.VMEM((2 * PIECE, HD), F32),
            pltpu.VMEM((PIECE, HD), F32),
            pltpu.VMEM((2 * PIECE, 2 * HD), F32),
            pltpu.VMEM((PIECE, 2 * HD), F32),
            pltpu.VMEM((2 * PIECE, HD), F32),
            dma((4, 4)),
            dma((4, 4)),
            dma((4, STEPS + 1, SUBS)),
            dma((32, SUBS)),
            dma((4, STEPS + 1)),
            dma((32,)),
            dma((4, SUBS + 1)),
            dma,
            dma((5,)),
            dma((5,)),
            dma((4,)),
            dma((4,)),
            dma((3, 4)),
            dma((3, 4)),
            dma((3,)),
            dma((4,)),
        ],
        compiler_params=pltpu.CompilerParams(collective_id=0, has_side_effects=True),
        name="attention",
    )(query_rows, key_rows, value_rows, out_weight, cluster_ids)
    return total.astype(BF16)


def solution(mesh):
    split = Mesh(
        mesh.devices.reshape(8, 8, 2, mesh.shape["head"]), ("seq_0", "seq_1", "seq_2", "head")
    )
    return jax.shard_map(
        body,
        mesh=split,
        in_specs=(P(SEQ, "head"), P(SEQ, "head"), P(SEQ, "head"), P("head", None), P(SEQ, None)),
        out_specs=P(SEQ, "head"),
        check_vma=False,
    )
```

```python
import jax
import jax.numpy as jnp
from jax import lax
from jax.experimental import pallas as pl
from jax.experimental.pallas import tpu as pltpu
from jax.sharding import Mesh
from jax.sharding import PartitionSpec as P

HD = 128
BLOCK = 8
WINDOW = 1024
SEQ = ("seq_0", "seq_1", "seq_2")
MESH = pl.DeviceIdType.MESH
TILE = 128
PIECE = 4 * TILE
SUBS = 4
STEPS = 4
NEG = -1e30
F32 = jnp.float32
BF16 = jnp.bfloat16


def kernel(
    q_in, k_in, v_in, w_in, id_in, out_ref,
    q_buf, slots, id_row, id_slots, o_buf, o_away, o_in, stats, stats_in, att, w_buf,
    m_r, m_l, acc_r, acc_l, q_id,
    u_send, u_recv, ag_send, ag_recv, id_send, id_recv, y_send, q_recv, o_send, o_recv,
    ret_send, ret_recv, x_send, x_recv, w_send, w_recv,
):
    z, y, c = (lax.axis_index(a) for a in SEQ)
    x = lax.axis_index("head")
    nz, ny, nx = lax.axis_size("seq_0"), lax.axis_size("seq_1"), lax.axis_size("head")
    par = y % 2
    mate = y + 1 - 2 * par
    twin = 1 - c
    piece = 4 * z + 2 * c + par
    place = 2 * ((y // 2) % 2) + c
    head = y // 2
    z_up, z_down = (z + 1) % nz, (z + nz - 1) % nz
    x_up, x_down, x_far = (x + 1) % nx, (x + nx - 1) % nx, (x + 2) % nx
    dests = [(y + far) % ny for far in (1, ny - 1, 3, ny - 3)]
    first = 2 * ((1 - par + 4 * c - y + 2 * ny) % ny == 5).astype(jnp.int32)
    sources = [(1 - par + 4 * c + 2 * (r // 2), r % 2) for r in range(4)]

    def remote(src, dst, send_sem, recv_sem, to):
        return pltpu.make_async_remote_copy(
            src_ref=src, dst_ref=dst, send_sem=send_sem, recv_sem=recv_sem,
            device_id=to, device_id_type=MESH,
        )

    here = (z, mate, c, x)

    def wait_recv(dst, sem):
        remote(dst, dst, sem, sem, here).wait_recv()

    def wait_send(src, sem):
        remote(src, src, sem, sem, here).wait_send()

    barrier = pltpu.get_barrier_semaphore()
    near = [(z, yy, y // 4, x) for yy in dests] + [(z, yy, cc, x) for yy, cc in sources]
    near += [(z_up, y, c, x), (z_down, y, c, x), (z, mate, c, x), (z, y, twin, x)]
    near += [(z, y, c, x_up), (z, y, c, x_down), (z, y, c, x_far)]
    for to in near:
        pl.semaphore_signal(barrier, 1, device_id=to, device_id_type=MESH)

    def w_columns(to):
        return w_in.at[:, pl.ds(pl.multiple_of(to * 4 * HD, 4 * HD), 4 * HD)]

    pltpu.make_async_copy(w_columns(x), w_buf.at[x], w_recv.at[0]).start()
    block_of = lax.broadcasted_iota(jnp.int32, (1, TILE), 1) // BLOCK
    row = jnp.zeros((1, TILE), jnp.int32)
    for b in range(TILE // BLOCK):
        row = jnp.where(block_of == b, id_in[0, b], row)
    id_row[...] = row
    m_r[...] = jnp.full_like(m_r, NEG)
    m_l[...] = jnp.full_like(m_l, NEG)
    acc_r[...] = jnp.zeros_like(acc_r)
    acc_l[...] = jnp.zeros_like(acc_l)

    pl.semaphore_wait(barrier, len(near))

    def rows_of(r):
        return pl.ds(pl.multiple_of(r * TILE, TILE), TILE)

    def landing(j, r):
        return [
            slots.at[j, rows_of(r), 0:HD],
            slots.at[j, rows_of(r), HD : 2 * HD],
            id_slots.at[j, r],
            q_buf.at[rows_of(r), :],
        ]

    def leaving(yy):
        lanes = pl.ds(pl.multiple_of((yy // 2) * HD, HD), HD)
        return [k_in.at[:, lanes], v_in.at[:, lanes], id_row, q_in.at[:, lanes]]

    for tensors in ((0, 1, 2), (3,)):
        for i, yy in enumerate(dests):
            landed = landing(4 * z + 2 * (y // 4) + (1 - par), place)
            for t in tensors:
                remote(
                    leaving(yy)[t], landed[t], u_send.at[i, t], u_recv.at[place, t],
                    (z, yy, y // 4, x),
                ).start()

    for d, to in enumerate((x_up, x_down, x_far)):
        remote(
            w_columns(to), w_buf.at[x], w_send.at[d], w_recv.at[1 + d], (z, y, c, to)
        ).start()

    def slot_of(dz, core, p):
        return 4 * ((z + dz + nz) % nz) + 2 * core + p

    def sub_of(j, sub):
        return slots.at[j, rows_of(sub), :]

    to_up, to_down, to_mate, to_twin = (z_up, y, c, x), (z_down, y, c, x), here, (z, y, twin, x)

    def send(j, sub, send_sem, to):
        ref = sub_of(j, sub)
        remote(ref, ref, send_sem, ag_recv.at[j, sub], to).start()

    def send_ids(j, send_sem, to):
        remote(id_slots.at[j], id_slots.at[j], send_sem, id_recv.at[j], to).start()

    def send_whole(j, n, to):
        send_ids(j, y_send.at[n, SUBS], to)
        for sub in range(SUBS):
            send(j, sub, y_send.at[n, sub], to)

    def wait_whole(j):
        wait_recv(id_slots.at[j], id_recv.at[j])
        for sub in range(SUBS):
            wait_recv(sub_of(j, sub), ag_recv.at[j, sub])

    for n in range(4):
        r = (first + n) % 4
        landed = landing(piece, r)
        for t in range(3):
            wait_recv(landed[t], u_recv.at[r, t])
        send(piece, r, ag_send.at[0, 1, r], to_up)
        send(piece, r, ag_send.at[1, 1, r], to_down)
        send(piece, r, ag_send.at[2, 0, r], to_twin)
    send_ids(piece, id_send.at[0, 1], to_up)
    send_ids(piece, id_send.at[1, 1], to_down)
    send_ids(piece, id_send.at[2, 0], to_twin)

    def forward(n, order):
        sub = (first + order) % 4
        low, high = slot_of(-n, c, par), slot_of(n, c, par)
        lower, upper = sub < 2, sub >= 2

        @pl.when((n < STEPS) | lower)
        def _():
            wait_recv(sub_of(low, sub), ag_recv.at[low, sub])

            @pl.when((n + 1 < STEPS) | ((n + 1 == STEPS) & lower))
            def _():
                send(low, sub, ag_send.at[0, n + 1, sub], to_up)

            send(low, sub, ag_send.at[2, n, sub], to_twin)

        @pl.when((n < STEPS) | upper)
        def _():
            wait_recv(sub_of(high, sub), ag_recv.at[high, sub])

            @pl.when((n + 1 < STEPS) | ((n + 1 == STEPS) & upper))
            def _():
                send(high, sub, ag_send.at[1, n + 1, sub], to_down)

            send(high, sub, ag_send.at[3, n, sub], to_twin)

        @pl.when(order == 0)
        def _():
            wait_recv(id_slots.at[low], id_recv.at[low])
            send_ids(low, id_send.at[2, n], to_twin)

            @pl.when(n < STEPS)
            def _():
                wait_recv(id_slots.at[high], id_recv.at[high])
                send_ids(low, id_send.at[0, n + 1], to_up)
                send_ids(high, id_send.at[3, n], to_twin)

                @pl.when(n + 1 < STEPS)
                def _():
                    send_ids(high, id_send.at[1, n + 1], to_down)

    def forward_first(order, carry):
        forward(jnp.int32(1), order)
        return carry

    lax.fori_loop(0, 2, forward_first, 0)

    own_q, mate_q = q_buf.at[0:PIECE, :], q_buf.at[PIECE : 2 * PIECE, :]
    for r in range(4):
        wait_recv(landing(piece, r)[3], u_recv.at[r, 3])
    remote(own_q, mate_q, y_send.at[0, 0], q_recv, to_mate).start()
    send_whole(piece, 1, to_mate)

    def ids_of(j):
        return jnp.concatenate([id_slots[j, r] for r in range(4)], axis=1).astype(F32)

    eye = lax.broadcasted_iota(jnp.int32, (TILE, TILE), 0) == lax.broadcasted_iota(
        jnp.int32, (TILE, TILE), 1
    )

    def column_from(row):
        column = jnp.sum(
            jnp.where(eye, jnp.broadcast_to(row, (TILE, TILE)), 0.0), axis=1, keepdims=True
        )
        return jnp.broadcast_to(column, (TILE, TILE))

    def row_from(column):
        return jnp.sum(jnp.where(eye, column, 0.0), axis=0, keepdims=True)

    def set_query_ids(first, j):
        found = ids_of(j)
        for r in range(4):
            q_id[first + r * TILE : first + (r + 1) * TILE, :] = column_from(
                found[:, r * TILE : (r + 1) * TILE]
            )

    set_query_ids(0, piece)

    factor = HD ** -0.5 * 1.4426950408889634

    def across_keys(col):
        return jnp.concatenate([col] * 4, axis=1)

    def accumulate(scores, values, rows, m_ref, acc_ref):
        before = m_ref[rows, :]
        after = jnp.maximum(before, jnp.max(scores, axis=1, keepdims=True))
        weights = jnp.exp2(scores - across_keys(after))
        kept = jnp.exp2(before - after)
        m_ref[rows, :] = after
        acc_ref[rows, :] = acc_ref[rows, :] * jnp.concatenate([kept, kept], axis=1) + jnp.dot(
            weights.astype(BF16), values, preferred_element_type=F32
        )

    def start_of(j):
        return 1024 * (j // 2) + 256 * (1 - j % 2)

    def attend(j, bases, kind):
        keys = slots[j, :, 0:HD]
        values = jnp.concatenate([slots[j, :, HD : 2 * HD], jnp.ones((PIECE, HD), BF16)], axis=1)
        key_ids = ids_of(j)
        lane = lax.broadcasted_iota(jnp.int32, (1, PIECE), 1)
        key_place = lane + jnp.where(lane >= 256, 256, 0) + (start_of(j) - start_of(piece))
        query_row = lax.broadcasted_iota(jnp.int32, (TILE, TILE), 0)
        for first_row in [base + r * TILE for base in bases for r in range(4)]:
            rows = slice(first_row, first_row + TILE)
            scores = lax.dot_general(
                q_buf[rows, :], keys, (((1,), (1,)), ((), ())), preferred_element_type=F32
            ) * factor
            if kind == "far":
                allowed = across_keys(q_id[rows, :]) == key_ids
            else:
                query_place = first_row + 256 * (first_row // 256)
                ahead = (key_place - query_place) - across_keys(query_row)
                allowed = ahead <= 0
                if kind == "near":
                    allowed = allowed & (across_keys(q_id[rows, :]) == key_ids)
                else:
                    allowed = allowed & (ahead > -WINDOW)
            scores = jnp.where(allowed, scores, NEG)
            if kind == "local":
                accumulate(scores, values, rows, m_l, acc_l)
            else:
                accumulate(scores, values, rows, m_r, acc_r)

    mate_piece = slot_of(0, c, 1 - par)
    before_mate = 2 * ((piece // 2 + 2 * nz - 1) % (2 * nz)) + 1 - par

    def turn(t, carry):
        s, k = t // 5, t % 5
        extra = k == 2
        order = jnp.where(s == 0, k + 2, k - (k > 2).astype(jnp.int32))
        moves = jnp.where(s == 0, k < 2, (s < STEPS) & (k != 2))
        from_twin = (k > 2).astype(jnp.int32)
        upward = (k == 1) | (k == 4)
        core = c + from_twin * (1 - 2 * c)
        j = slot_of(jnp.where(upward, s, -s), core, par)
        j = jnp.where(extra, jnp.where(s == 2, mate_piece, before_mate), j)
        used = jnp.where(extra, (s == 2) | (s == 3), jnp.logical_not(upward) | ((s > 0) & (s < 4)))

        @pl.when((s == 1) & moves)
        def _():
            forward(s + 1, order)

        @pl.when(t == 5)
        def _():
            wait_recv(mate_q, q_recv)
            wait_recv(id_slots.at[mate_piece], id_recv.at[mate_piece])
            set_query_ids(PIECE, mate_piece)

        @pl.when(used & (from_twin == 1))
        def _():
            wait_whole(j)

        @pl.when((s == 1) & (k == 3) & (c == 0))
        def _():
            send_whole(j, 2, to_mate)

        @pl.when(extra & (s == 2))
        def _():
            for sub in range(SUBS):
                wait_recv(sub_of(j, sub), ag_recv.at[j, sub])

            @pl.when(c == 0)
            def _():
                send_whole(j, 3, to_twin)

        @pl.when(extra & (s == 3))
        def _():
            wait_whole(j)

        back = piece // 2 - j // 2

        @pl.when(used & (back >= 0) & (back <= 1))
        def _():
            attend(j, (0,), "near")

        @pl.when(used & (back > 1))
        def _():
            attend(j, (PIECE, 0), "far")

        @pl.when((s != 1) & moves)
        def _():
            forward(s + 1, order)

        return carry

    lax.fori_loop(0, 5 * STEPS, turn, 0)

    last_own, last_twin = slot_of(STEPS, c, par), slot_of(STEPS, twin, par)

    def attend_far(j, base):
        @pl.when(piece // 2 - j // 2 > 1)
        def _():
            attend(j, (base,), "far")

    attend_far(last_own, PIECE)
    attend_far(last_own, 0)
    wait_whole(last_twin)
    attend_far(last_twin, PIECE)

    for r in range(4):
        rows = slice(PIECE + r * TILE, PIECE + (r + 1) * TILE)
        stats[2 * r : 2 * r + 1, :] = row_from(m_r[rows, :])
        stats[2 * r + 1 : 2 * r + 2, :] = row_from(acc_r[rows, HD : 2 * HD])
    remote(stats, stats_in, o_send.at[4], o_recv.at[4], to_mate).start()
    for r in range(4):
        rows = slice(PIECE + r * TILE, PIECE + (r + 1) * TILE)
        here_rows = slice(r * TILE, (r + 1) * TILE)
        weight = jnp.maximum(acc_r[rows, HD : 2 * HD], 1e-30)
        o_away[here_rows, :] = (acc_r[rows, 0:HD] / weight).astype(BF16)
        remote(
            o_away.at[here_rows, :], o_in.at[here_rows, :], o_send.at[r], o_recv.at[r], to_mate
        ).start()
    attend_far(last_twin, 0)

    def attend_local(n, carry):
        half = piece // 2 - n // 2
        j = 2 * jnp.maximum(half, 0) + (par + n) % 2

        @pl.when(half >= 0)
        def _():
            attend(j, (0,), "local")

        return carry

    lax.fori_loop(0, 4, attend_local, 0)
    wait_recv(stats_in, o_recv.at[4])

    columns = pl.ds(pl.multiple_of(head * HD, HD), HD)
    for r, (yy, cc) in enumerate(sources):
        rows = slice(r * TILE, (r + 1) * TILE)
        wait_recv(o_in.at[rows, :], o_recv.at[r])
        m_here, m_there = m_r[rows, :], column_from(stats_in[2 * r : 2 * r + 1, :])
        largest = jnp.maximum(m_here, m_there)
        kept = jnp.exp2(m_here - largest)
        added = jnp.exp2(m_there - largest) * column_from(stats_in[2 * r + 1 : 2 * r + 2, :])
        routed = (acc_r[rows, 0:HD] * kept + o_in[rows, :].astype(F32) * added) / (
            acc_r[rows, HD : 2 * HD] * kept + added
        )
        routed = routed.astype(BF16).astype(F32)
        local = acc_l[rows, 0:HD] / acc_l[rows, HD : 2 * HD]
        o_buf[rows, :] = (routed + local).astype(BF16)
        remote(
            o_buf.at[rows, :], att.at[x, :, columns], ret_send.at[r], ret_recv.at[head],
            (z, yy, cc, x),
        ).start()

    def block(plane, n):
        lanes = pl.ds(pl.multiple_of((dests[n] // 2) * HD, HD), HD)
        return att.at[plane, :, lanes]

    def pass_on(plane, n, way, slot, to):
        ref = block(plane, n)
        remote(ref, ref, x_send.at[way, n], x_recv.at[slot, n], (z, y, c, to)).start()

    def project(plane):
        return jnp.dot(att[plane], w_buf[plane], preferred_element_type=F32)

    for n in range(4):
        wait_recv(block(x, n), ret_recv.at[dests[n] // 2])
        pass_on(x, n, 0, 0, x_up)
        pass_on(x, n, 1, 1, x_down)
    for d, plane in enumerate((x, x_down, x_up, x_far)):
        wait_recv(w_buf.at[plane], w_recv.at[d])
    total = project(x)
    for n in range(4):
        if n % 2 == 0:
            wait_recv(block(x_down, n), x_recv.at[0, n])
            pass_on(x_down, n, 2, 2, x_up)
        else:
            wait_recv(block(x_up, n), x_recv.at[1, n])
            pass_on(x_up, n, 2, 2, x_down)
    for n in (1, 3):
        wait_recv(block(x_down, n), x_recv.at[0, n])
    total = total + project(x_down)
    for n in (0, 2):
        wait_recv(block(x_up, n), x_recv.at[1, n])
    total = total + project(x_up)
    for n in range(4):
        wait_recv(block(x_far, n), x_recv.at[2, n])
    out_ref[...] = total + project(x_far)

    for i, yy in enumerate(dests):
        for t, ref in enumerate(leaving(yy)):
            wait_send(ref, u_send.at[i, t])
    for r in range(4):
        wait_send(o_buf.at[r * TILE : (r + 1) * TILE, :], ret_send.at[r])
    for r in range(4):
        wait_send(o_away.at[r * TILE : (r + 1) * TILE, :], o_send.at[r])
    wait_send(stats, o_send.at[4])
    wait_send(own_q, y_send.at[0, 0])

    def sent_whole(n):
        for sub in range(SUBS):
            wait_send(sub_of(0, sub), y_send.at[n, sub])
        wait_send(id_slots.at[0], y_send.at[n, SUBS])

    sent_whole(1)

    @pl.when(c == 0)
    def _():
        sent_whole(2)
        sent_whole(3)

    wait_send(id_slots.at[0], id_send.at[2, 0])
    for sub in range(SUBS):
        wait_send(sub_of(0, sub), ag_send.at[2, 0, sub])

    def settle(s, carry):
        for d in range(4):
            wait_send(id_slots.at[0], id_send.at[d, s])
            for sub in range(SUBS):
                wait_send(sub_of(0, sub), ag_send.at[d, s, sub])
        return carry

    lax.fori_loop(1, STEPS, settle, 0)
    for d in (0, 2):
        wait_send(id_slots.at[0], id_send.at[d, STEPS])
    for d in range(4):
        for sub in range(2):
            n = sub + 2 * (d % 2)
            wait_send(sub_of(0, n), ag_send.at[d, STEPS, n])
    for d in range(3):
        wait_send(w_buf.at[0], w_send.at[d])
        for n in range(4):
            wait_send(block(0, n), x_send.at[d, n])


def body(query_rows, key_rows, value_rows, out_weight, cluster_ids):
    tokens, width = query_rows.shape
    dma = pltpu.SemaphoreType.DMA
    anywhere = pl.BlockSpec(memory_space=pl.ANY)
    total = pl.pallas_call(
        kernel,
        out_shape=jax.ShapeDtypeStruct((tokens, width), F32),
        in_specs=[anywhere] * 4 + [pl.BlockSpec(memory_space=pltpu.SMEM)],
        out_specs=pl.BlockSpec(memory_space=pltpu.VMEM),
        scratch_shapes=[
            pltpu.VMEM((2 * PIECE, HD), BF16),
            pltpu.VMEM((32, PIECE, 2 * HD), BF16),
            pltpu.VMEM((1, TILE), jnp.int32),
            pltpu.VMEM((32, 4, 1, TILE), jnp.int32),
            pltpu.VMEM((PIECE, HD), BF16),
            pltpu.VMEM((PIECE, HD), BF16),
            pltpu.VMEM((PIECE, HD), BF16),
            pltpu.VMEM((8, TILE), F32),
            pltpu.VMEM((8, TILE), F32),
            pltpu.VMEM((4, tokens, width), BF16),
            pltpu.VMEM((4, width, width), BF16),
            pltpu.VMEM((2 * PIECE, HD), F32),
            pltpu.VMEM((PIECE, HD), F32),
            pltpu.VMEM((2 * PIECE, 2 * HD), F32),
            pltpu.VMEM((PIECE, 2 * HD), F32),
            pltpu.VMEM((2 * PIECE, HD), F32),
            dma((4, 4)),
            dma((4, 4)),
            dma((4, STEPS + 1, SUBS)),
            dma((32, SUBS)),
            dma((4, STEPS + 1)),
            dma((32,)),
            dma((4, SUBS + 1)),
            dma,
            dma((5,)),
            dma((5,)),
            dma((4,)),
            dma((4,)),
            dma((3, 4)),
            dma((3, 4)),
            dma((3,)),
            dma((4,)),
        ],
        compiler_params=pltpu.CompilerParams(collective_id=0, has_side_effects=True),
        name="attention",
    )(query_rows, key_rows, value_rows, out_weight, cluster_ids)
    return total.astype(BF16)


def solution(mesh):
    split = Mesh(
        mesh.devices.reshape(8, 8, 2, mesh.shape["head"]), ("seq_0", "seq_1", "seq_2", "head")
    )
    return jax.shard_map(
        body,
        mesh=split,
        in_specs=(P(SEQ, "head"), P(SEQ, "head"), P(SEQ, "head"), P("head", None), P(SEQ, None)),
        out_specs=P(SEQ, "head"),
        check_vma=False,
    )
```

```python
import jax
import jax.numpy as jnp
from jax import lax
from jax.experimental import pallas as pl
from jax.experimental.pallas import tpu as pltpu
from jax.sharding import Mesh
from jax.sharding import PartitionSpec as P

HD = 128
BLOCK = 8
WINDOW = 1024
SEQ = ("seq_0", "seq_1", "seq_2")
MESH = pl.DeviceIdType.MESH
TILE = 128
PIECE = 4 * TILE
SUBS = 4
STEPS = 4
NEG = -1e30
F32 = jnp.float32
BF16 = jnp.bfloat16


def kernel(
    q_in, k_in, v_in, w_in, id_in, out_ref,
    q_buf, slots, id_row, id_slots, o_buf, o_away, o_in, stats, stats_in, att, w_buf,
    m_r, m_l, acc_r, acc_l, q_id,
    u_send, u_recv, ag_send, ag_recv, id_send, id_recv, y_send, q_recv, o_send, o_recv,
    ret_send, ret_recv, x_send, x_recv, w_send, w_recv,
):
    z, y, c = (lax.axis_index(a) for a in SEQ)
    x = lax.axis_index("head")
    nz, ny, nx = lax.axis_size("seq_0"), lax.axis_size("seq_1"), lax.axis_size("head")
    par = y % 2
    mate = y + 1 - 2 * par
    twin = 1 - c
    piece = 4 * z + 2 * c + par
    place = 2 * ((y // 2) % 2) + c
    head = y // 2
    z_up, z_down = (z + 1) % nz, (z + nz - 1) % nz
    x_up, x_down, x_far = (x + 1) % nx, (x + nx - 1) % nx, (x + 2) % nx
    dests = [(y + far) % ny for far in (1, ny - 1, 3, ny - 3)]
    first = 2 * ((1 - par + 4 * c - y + 2 * ny) % ny == 5).astype(jnp.int32)
    sources = [(1 - par + 4 * c + 2 * (r // 2), r % 2) for r in range(4)]

    def remote(src, dst, send_sem, recv_sem, to):
        return pltpu.make_async_remote_copy(
            src_ref=src, dst_ref=dst, send_sem=send_sem, recv_sem=recv_sem,
            device_id=to, device_id_type=MESH,
        )

    here = (z, mate, c, x)

    def wait_recv(dst, sem):
        remote(dst, dst, sem, sem, here).wait_recv()

    def wait_send(src, sem):
        remote(src, src, sem, sem, here).wait_send()

    barrier = pltpu.get_barrier_semaphore()
    near = [(z, yy, y // 4, x) for yy in dests] + [(z, yy, cc, x) for yy, cc in sources]
    near += [(z_up, y, c, x), (z_down, y, c, x), (z, mate, c, x), (z, y, twin, x)]
    near += [(z, y, c, x_up), (z, y, c, x_down), (z, y, c, x_far)]
    for to in near:
        pl.semaphore_signal(barrier, 1, device_id=to, device_id_type=MESH)

    def w_columns(to):
        return w_in.at[:, pl.ds(pl.multiple_of(to * 4 * HD, 4 * HD), 4 * HD)]

    pltpu.make_async_copy(w_columns(x), w_buf.at[x], w_recv.at[0]).start()
    block_of = lax.broadcasted_iota(jnp.int32, (1, TILE), 1) // BLOCK
    row = jnp.zeros((1, TILE), jnp.int32)
    for b in range(TILE // BLOCK):
        row = jnp.where(block_of == b, id_in[0, b], row)
    id_row[...] = row
    m_r[...] = jnp.full_like(m_r, NEG)
    m_l[...] = jnp.full_like(m_l, NEG)
    acc_r[...] = jnp.zeros_like(acc_r)
    acc_l[...] = jnp.zeros_like(acc_l)

    pl.semaphore_wait(barrier, len(near))

    def rows_of(r):
        return pl.ds(pl.multiple_of(r * TILE, TILE), TILE)

    def landing(j, r):
        return [
            slots.at[j, rows_of(r), 0:HD],
            slots.at[j, rows_of(r), HD : 2 * HD],
            id_slots.at[j, r],
            q_buf.at[rows_of(r), :],
        ]

    def leaving(yy):
        lanes = pl.ds(pl.multiple_of((yy // 2) * HD, HD), HD)
        return [k_in.at[:, lanes], v_in.at[:, lanes], id_row, q_in.at[:, lanes]]

    for tensors in ((0, 1, 2), (3,)):
        for i, yy in enumerate(dests):
            landed = landing(4 * z + 2 * (y // 4) + (1 - par), place)
            for t in tensors:
                remote(
                    leaving(yy)[t], landed[t], u_send.at[i, t], u_recv.at[place, t],
                    (z, yy, y // 4, x),
                ).start()

    for d, to in enumerate((x_up, x_down, x_far)):
        remote(
            w_columns(to), w_buf.at[x], w_send.at[d], w_recv.at[1 + d], (z, y, c, to)
        ).start()

    def slot_of(dz, core, p):
        return 4 * ((z + dz + nz) % nz) + 2 * core + p

    def sub_of(j, sub):
        return slots.at[j, rows_of(sub), :]

    to_up, to_down, to_mate, to_twin = (z_up, y, c, x), (z_down, y, c, x), here, (z, y, twin, x)

    def send(j, sub, send_sem, to):
        ref = sub_of(j, sub)
        remote(ref, ref, send_sem, ag_recv.at[j, sub], to).start()

    def send_ids(j, send_sem, to):
        remote(id_slots.at[j], id_slots.at[j], send_sem, id_recv.at[j], to).start()

    def send_whole(j, n, to):
        send_ids(j, y_send.at[n, SUBS], to)
        for sub in range(SUBS):
            send(j, sub, y_send.at[n, sub], to)

    def wait_whole(j):
        wait_recv(id_slots.at[j], id_recv.at[j])
        for sub in range(SUBS):
            wait_recv(sub_of(j, sub), ag_recv.at[j, sub])

    for n in range(4):
        r = (first + n) % 4
        landed = landing(piece, r)
        for t in range(3):
            wait_recv(landed[t], u_recv.at[r, t])
        send(piece, r, ag_send.at[0, 1, r], to_up)
        send(piece, r, ag_send.at[1, 1, r], to_down)
        send(piece, r, ag_send.at[2, 0, r], to_twin)
    send_ids(piece, id_send.at[0, 1], to_up)
    send_ids(piece, id_send.at[1, 1], to_down)
    send_ids(piece, id_send.at[2, 0], to_twin)

    def forward(n, order):
        sub = (first + order) % 4
        low, high = slot_of(-n, c, par), slot_of(n, c, par)
        lower, upper = sub < 2, sub >= 2

        @pl.when((n < STEPS) | lower)
        def _():
            wait_recv(sub_of(low, sub), ag_recv.at[low, sub])

            @pl.when((n + 1 < STEPS) | ((n + 1 == STEPS) & lower))
            def _():
                send(low, sub, ag_send.at[0, n + 1, sub], to_up)

            send(low, sub, ag_send.at[2, n, sub], to_twin)

        @pl.when((n < STEPS) | upper)
        def _():
            wait_recv(sub_of(high, sub), ag_recv.at[high, sub])

            @pl.when((n + 1 < STEPS) | ((n + 1 == STEPS) & upper))
            def _():
                send(high, sub, ag_send.at[1, n + 1, sub], to_down)

            send(high, sub, ag_send.at[3, n, sub], to_twin)

        @pl.when(order == 0)
        def _():
            wait_recv(id_slots.at[low], id_recv.at[low])
            send_ids(low, id_send.at[2, n], to_twin)

            @pl.when(n < STEPS)
            def _():
                wait_recv(id_slots.at[high], id_recv.at[high])
                send_ids(low, id_send.at[0, n + 1], to_up)
                send_ids(high, id_send.at[3, n], to_twin)

                @pl.when(n + 1 < STEPS)
                def _():
                    send_ids(high, id_send.at[1, n + 1], to_down)

    def forward_first(order, carry):
        forward(jnp.int32(1), order)
        return carry

    lax.fori_loop(0, 2, forward_first, 0)

    own_q, mate_q = q_buf.at[0:PIECE, :], q_buf.at[PIECE : 2 * PIECE, :]
    for r in range(4):
        wait_recv(landing(piece, r)[3], u_recv.at[r, 3])
    remote(own_q, mate_q, y_send.at[0, 0], q_recv, to_mate).start()
    send_whole(piece, 1, to_mate)

    def ids_of(j):
        return jnp.concatenate([id_slots[j, r] for r in range(4)], axis=1).astype(F32)

    eye = lax.broadcasted_iota(jnp.int32, (TILE, TILE), 0) == lax.broadcasted_iota(
        jnp.int32, (TILE, TILE), 1
    )

    def column_from(row):
        column = jnp.sum(
            jnp.where(eye, jnp.broadcast_to(row, (TILE, TILE)), 0.0), axis=1, keepdims=True
        )
        return jnp.broadcast_to(column, (TILE, TILE))

    def row_from(column):
        return jnp.sum(jnp.where(eye, column, 0.0), axis=0, keepdims=True)

    def set_query_ids(first, j):
        found = ids_of(j)
        for r in range(4):
            q_id[first + r * TILE : first + (r + 1) * TILE, :] = column_from(
                found[:, r * TILE : (r + 1) * TILE]
            )

    set_query_ids(0, piece)

    factor = HD ** -0.5 * 1.4426950408889634

    def across_keys(col):
        return jnp.concatenate([col] * 4, axis=1)

    def accumulate(scores, values, rows, m_ref, acc_ref):
        before = m_ref[rows, :]
        after = jnp.maximum(before, jnp.max(scores, axis=1, keepdims=True))
        weights = jnp.exp2(scores - across_keys(after))
        kept = jnp.exp2(before - after)
        m_ref[rows, :] = after
        acc_ref[rows, :] = acc_ref[rows, :] * jnp.concatenate([kept, kept], axis=1) + jnp.dot(
            weights.astype(BF16), values, preferred_element_type=F32
        )

    def start_of(j):
        return 1024 * (j // 2) + 256 * (1 - j % 2)

    def attend(j, bases, kind):
        keys = slots[j, :, 0:HD]
        values = jnp.concatenate([slots[j, :, HD : 2 * HD], jnp.ones((PIECE, HD), BF16)], axis=1)
        key_ids = ids_of(j)
        lane = lax.broadcasted_iota(jnp.int32, (1, PIECE), 1)
        key_place = lane + jnp.where(lane >= 256, 256, 0) + (start_of(j) - start_of(piece))
        query_row = lax.broadcasted_iota(jnp.int32, (TILE, TILE), 0)
        for first_row in [base + r * TILE for base in bases for r in range(4)]:
            rows = slice(first_row, first_row + TILE)
            scores = lax.dot_general(
                q_buf[rows, :], keys, (((1,), (1,)), ((), ())), preferred_element_type=F32
            ) * factor
            if kind == "far":
                allowed = across_keys(q_id[rows, :]) == key_ids
            else:
                query_place = first_row + 256 * (first_row // 256)
                ahead = (key_place - query_place) - across_keys(query_row)
                allowed = ahead <= 0
                if kind == "near":
                    allowed = allowed & (across_keys(q_id[rows, :]) == key_ids)
                else:
                    allowed = allowed & (ahead > -WINDOW)
            scores = jnp.where(allowed, scores, NEG)
            if kind == "local":
                accumulate(scores, values, rows, m_l, acc_l)
            else:
                accumulate(scores, values, rows, m_r, acc_r)

    mate_piece = slot_of(0, c, 1 - par)
    before_mate = 2 * ((piece // 2 + 2 * nz - 1) % (2 * nz)) + 1 - par

    def turn(t, carry):
        s, k = t // 5, t % 5
        extra = k == 2
        order = jnp.where(s == 0, k + 2, k - (k > 2).astype(jnp.int32))
        moves = jnp.where(s == 0, k < 2, (s < STEPS) & (k != 2))
        from_twin = (k > 2).astype(jnp.int32)
        upward = (k == 1) | (k == 4)
        core = c + from_twin * (1 - 2 * c)
        j = slot_of(jnp.where(upward, s, -s), core, par)
        j = jnp.where(extra, jnp.where(s == 2, mate_piece, before_mate), j)
        used = jnp.where(extra, (s == 2) | (s == 3), jnp.logical_not(upward) | ((s > 0) & (s < 4)))

        @pl.when((s == 1) & moves)
        def _():
            forward(s + 1, order)

        @pl.when(t == 5)
        def _():
            wait_recv(mate_q, q_recv)
            wait_recv(id_slots.at[mate_piece], id_recv.at[mate_piece])
            set_query_ids(PIECE, mate_piece)

        @pl.when(used & (from_twin == 1))
        def _():
            wait_whole(j)

        @pl.when((s == 1) & (k == 3) & (c == 0))
        def _():
            send_whole(j, 2, to_mate)

        @pl.when(extra & (s == 2))
        def _():
            for sub in range(SUBS):
                wait_recv(sub_of(j, sub), ag_recv.at[j, sub])

            @pl.when(c == 0)
            def _():
                send_whole(j, 3, to_twin)

        @pl.when(extra & (s == 3))
        def _():
            wait_whole(j)

        back = piece // 2 - j // 2

        @pl.when(used & (back >= 0) & (back <= 1))
        def _():
            attend(j, (0,), "near")

            @pl.when(jnp.logical_not(extra))
            def _():
                attend(j, (0,), "local")

        @pl.when(used & (back > 1))
        def _():
            attend(j, (PIECE, 0), "far")

        @pl.when((s != 1) & moves)
        def _():
            forward(s + 1, order)

        return carry

    lax.fori_loop(0, 5 * STEPS, turn, 0)

    last_own, last_twin = slot_of(STEPS, c, par), slot_of(STEPS, twin, par)

    def attend_far(j, base):
        @pl.when(piece // 2 - j // 2 > 1)
        def _():
            attend(j, (base,), "far")

    attend_far(last_own, PIECE)
    attend_far(last_own, 0)
    wait_whole(last_twin)
    attend_far(last_twin, PIECE)

    for r in range(4):
        rows = slice(PIECE + r * TILE, PIECE + (r + 1) * TILE)
        stats[2 * r : 2 * r + 1, :] = row_from(m_r[rows, :])
        stats[2 * r + 1 : 2 * r + 2, :] = row_from(acc_r[rows, HD : 2 * HD])
    remote(stats, stats_in, o_send.at[4], o_recv.at[4], to_mate).start()
    for r in range(4):
        rows = slice(PIECE + r * TILE, PIECE + (r + 1) * TILE)
        here_rows = slice(r * TILE, (r + 1) * TILE)
        weight = jnp.maximum(acc_r[rows, HD : 2 * HD], 1e-30)
        o_away[here_rows, :] = (acc_r[rows, 0:HD] / weight).astype(BF16)
        remote(
            o_away.at[here_rows, :], o_in.at[here_rows, :], o_send.at[r], o_recv.at[r], to_mate
        ).start()
    attend_far(last_twin, 0)

    def attend_local(n, carry):
        half = piece // 2 - n
        j = 2 * jnp.maximum(half, 0) + 1 - par

        @pl.when(half >= 0)
        def _():
            attend(j, (0,), "local")

        return carry

    lax.fori_loop(0, 2, attend_local, 0)
    wait_recv(stats_in, o_recv.at[4])

    columns = pl.ds(pl.multiple_of(head * HD, HD), HD)
    for r, (yy, cc) in enumerate(sources):
        rows = slice(r * TILE, (r + 1) * TILE)
        wait_recv(o_in.at[rows, :], o_recv.at[r])
        m_here, m_there = m_r[rows, :], column_from(stats_in[2 * r : 2 * r + 1, :])
        largest = jnp.maximum(m_here, m_there)
        kept = jnp.exp2(m_here - largest)
        added = jnp.exp2(m_there - largest) * column_from(stats_in[2 * r + 1 : 2 * r + 2, :])
        routed = (acc_r[rows, 0:HD] * kept + o_in[rows, :].astype(F32) * added) / (
            acc_r[rows, HD : 2 * HD] * kept + added
        )
        routed = routed.astype(BF16).astype(F32)
        local = acc_l[rows, 0:HD] / acc_l[rows, HD : 2 * HD]
        o_buf[rows, :] = (routed + local).astype(BF16)
        remote(
            o_buf.at[rows, :], att.at[x, :, columns], ret_send.at[r], ret_recv.at[head],
            (z, yy, cc, x),
        ).start()

    def block(plane, n):
        lanes = pl.ds(pl.multiple_of((dests[n] // 2) * HD, HD), HD)
        return att.at[plane, :, lanes]

    def pass_on(plane, n, way, slot, to):
        ref = block(plane, n)
        remote(ref, ref, x_send.at[way, n], x_recv.at[slot, n], (z, y, c, to)).start()

    def project(plane):
        return jnp.dot(att[plane], w_buf[plane], preferred_element_type=F32)

    for n in range(4):
        wait_recv(block(x, n), ret_recv.at[dests[n] // 2])
        pass_on(x, n, 0, 0, x_up)
        pass_on(x, n, 1, 1, x_down)
    for d, plane in enumerate((x, x_down, x_up, x_far)):
        wait_recv(w_buf.at[plane], w_recv.at[d])
    total = project(x)
    for n in range(4):
        if n % 2 == 0:
            wait_recv(block(x_down, n), x_recv.at[0, n])
            pass_on(x_down, n, 2, 2, x_up)
        else:
            wait_recv(block(x_up, n), x_recv.at[1, n])
            pass_on(x_up, n, 2, 2, x_down)
    for n in (1, 3):
        wait_recv(block(x_down, n), x_recv.at[0, n])
    total = total + project(x_down)
    for n in (0, 2):
        wait_recv(block(x_up, n), x_recv.at[1, n])
    total = total + project(x_up)
    for n in range(4):
        wait_recv(block(x_far, n), x_recv.at[2, n])
    out_ref[...] = total + project(x_far)

    for i, yy in enumerate(dests):
        for t, ref in enumerate(leaving(yy)):
            wait_send(ref, u_send.at[i, t])
    for r in range(4):
        wait_send(o_buf.at[r * TILE : (r + 1) * TILE, :], ret_send.at[r])
    for r in range(4):
        wait_send(o_away.at[r * TILE : (r + 1) * TILE, :], o_send.at[r])
    wait_send(stats, o_send.at[4])
    wait_send(own_q, y_send.at[0, 0])

    def sent_whole(n):
        for sub in range(SUBS):
            wait_send(sub_of(0, sub), y_send.at[n, sub])
        wait_send(id_slots.at[0], y_send.at[n, SUBS])

    sent_whole(1)

    @pl.when(c == 0)
    def _():
        sent_whole(2)
        sent_whole(3)

    wait_send(id_slots.at[0], id_send.at[2, 0])
    for sub in range(SUBS):
        wait_send(sub_of(0, sub), ag_send.at[2, 0, sub])

    def settle(s, carry):
        for d in range(4):
            wait_send(id_slots.at[0], id_send.at[d, s])
            for sub in range(SUBS):
                wait_send(sub_of(0, sub), ag_send.at[d, s, sub])
        return carry

    lax.fori_loop(1, STEPS, settle, 0)
    for d in (0, 2):
        wait_send(id_slots.at[0], id_send.at[d, STEPS])
    for d in range(4):
        for sub in range(2):
            n = sub + 2 * (d % 2)
            wait_send(sub_of(0, n), ag_send.at[d, STEPS, n])
    for d in range(3):
        wait_send(w_buf.at[0], w_send.at[d])
        for n in range(4):
            wait_send(block(0, n), x_send.at[d, n])


def body(query_rows, key_rows, value_rows, out_weight, cluster_ids):
    tokens, width = query_rows.shape
    dma = pltpu.SemaphoreType.DMA
    anywhere = pl.BlockSpec(memory_space=pl.ANY)
    total = pl.pallas_call(
        kernel,
        out_shape=jax.ShapeDtypeStruct((tokens, width), F32),
        in_specs=[anywhere] * 4 + [pl.BlockSpec(memory_space=pltpu.SMEM)],
        out_specs=pl.BlockSpec(memory_space=pltpu.VMEM),
        scratch_shapes=[
            pltpu.VMEM((2 * PIECE, HD), BF16),
            pltpu.VMEM((32, PIECE, 2 * HD), BF16),
            pltpu.VMEM((1, TILE), jnp.int32),
            pltpu.VMEM((32, 4, 1, TILE), jnp.int32),
            pltpu.VMEM((PIECE, HD), BF16),
            pltpu.VMEM((PIECE, HD), BF16),
            pltpu.VMEM((PIECE, HD), BF16),
            pltpu.VMEM((8, TILE), F32),
            pltpu.VMEM((8, TILE), F32),
            pltpu.VMEM((4, tokens, width), BF16),
            pltpu.VMEM((4, width, width), BF16),
            pltpu.VMEM((2 * PIECE, HD), F32),
            pltpu.VMEM((PIECE, HD), F32),
            pltpu.VMEM((2 * PIECE, 2 * HD), F32),
            pltpu.VMEM((PIECE, 2 * HD), F32),
            pltpu.VMEM((2 * PIECE, HD), F32),
            dma((4, 4)),
            dma((4, 4)),
            dma((4, STEPS + 1, SUBS)),
            dma((32, SUBS)),
            dma((4, STEPS + 1)),
            dma((32,)),
            dma((4, SUBS + 1)),
            dma,
            dma((5,)),
            dma((5,)),
            dma((4,)),
            dma((4,)),
            dma((3, 4)),
            dma((3, 4)),
            dma((3,)),
            dma((4,)),
        ],
        compiler_params=pltpu.CompilerParams(collective_id=0, has_side_effects=True),
        name="attention",
    )(query_rows, key_rows, value_rows, out_weight, cluster_ids)
    return total.astype(BF16)


def solution(mesh):
    split = Mesh(
        mesh.devices.reshape(8, 8, 2, mesh.shape["head"]), ("seq_0", "seq_1", "seq_2", "head")
    )
    return jax.shard_map(
        body,
        mesh=split,
        in_specs=(P(SEQ, "head"), P(SEQ, "head"), P(SEQ, "head"), P("head", None), P(SEQ, None)),
        out_specs=P(SEQ, "head"),
        check_vma=False,
    )
```
